256 devices in a mesh: dp: 4 (over x), expert: 64 (over y, z, core).
Axes of the slice: x: 4, y: 4, z: 8, core: 2. Of those that a mesh axis runs over, the one named last changes fastest.
Arguments:
- tokens: bfloat16 [32768, 2048], P(('dp', 'expert')), may hold values from -6 to 6
- out_grad: bfloat16 [32768, 2048], P(('dp', 'expert')), may hold values from -6 to 6
- gate_probs: bfloat16 [32768, 4], P(('dp', 'expert')), may hold values from 0.049804688 to 0.59765625
- expert_ids: int32 [32768, 4], P(('dp', 'expert')), may hold values from 0 to 63, all different within a row; in each aligned block of 128 rows (0 to 127, 128 to 255, ...) at most 9 rows name the same one
- w_gate: bfloat16 [64, 2048, 768], P('expert'), may hold values from -0.125 to 0.125
- w_up: bfloat16 [64, 2048, 768], P('expert'), may hold values from -0.125 to 0.125
- w_down: bfloat16 [64, 768, 2048], P('expert'), may hold values from -0.21875 to 0.21875
Outputs:
- tokens_grad: bfloat16 [32768, 2048], P(('dp', 'expert'))
- probs_grad: float32 [32768, 4], P(('dp', 'expert'))
- gate_weight_grad: bfloat16 [64, 2048, 768], P('expert', None, 'dp')
- up_weight_grad: bfloat16 [64, 2048, 768], P('expert', None, 'dp')
- down_weight_grad: bfloat16 [64, 768, 2048], P('expert', 'dp')
The draws below stay inside these ranges and needn't reach their ends.
Inputs may be any that keep to these rules, and one draw needn't show every extreme that they name: `expert_ids`: each row names 4 different experts. In each aligned block of 128 rows (the rows of one device) no expert is named by more than 9 rows, a bound that some block reaches.
All inputs are finite; a program needn't handle non-finite values.
Results may differ from the reference program's by a relative error of at most 0.0057.
Values may be sent and summed in bfloat16 or wider, within the bound.
No kernel may reach another device: no remote copies, remote signals or barrier semaphores. Data moves between devices by JAX's collectives and lax.ppermute only.
A program may use at most 192 MiB of HBM per device.

```python
import math
import jax
import jax.numpy as jnp
import numpy as np
from jax import lax

D = 2048
H = 768
TOP = 4
TOK_DEV = 128
EXPERTS = 64
TOKENS = 32768
CAP = 9
N_DP = 4
N_EXPERT = 64


def block_levels(stream_key, shape, split, smallest, largest):
    loudness = 1.0
    for axis_at, shards_of in split:
        draws = jax.random.uniform(jax.random.fold_in(jax.random.fold_in(stream_key, 6), axis_at), (shards_of,), jnp.float32, smallest / len(split), largest / len(split))
        loudness = loudness * jnp.repeat(jnp.exp(draws), shape[axis_at] // shards_of).reshape((-1,) + (1,) * (len(shape) - 1 - axis_at))
    return loudness


def deal_out(stream_key, own, number, rows, count, top, bound, slope):
    order = jax.random.permutation(stream_key, count)
    packed, usual = load_shares(count, rows * top, bound, slope, True), load_shares(count, rows * top, bound, slope, False)
    places = jnp.arange(count)

    def named(lengths, turn):
        used = int((lengths > 0).sum())
        fixed = max(1, used // 4)
        passed = fixed + (places - fixed + turn * (used - fixed)) % max(1, count - fixed)
        return jnp.zeros((count,), jnp.int32).at[order[jnp.where(places < fixed, places, passed)]].set(jnp.asarray(lengths, jnp.int32))

    lengths = jnp.where(number % 4 == 0, named(packed, number // 4), named(usual, number - number // 4 - 1))
    mixed = jax.random.permutation(jax.random.fold_in(own, 3), count)
    donor, sink = mixed[0:count // 2 * 2:2], mixed[1:count // 2 * 2:2]
    slack = jnp.minimum(lengths[donor] - 1, bound - lengths[sink]) // 2
    slack = jnp.where((donor == order[0]) | (sink == order[0]) | (lengths[sink] == 0), 0, jnp.maximum(slack, 0))
    passed = jax.random.randint(jax.random.fold_in(own, 4), (count // 2,), 0, 1 << 20) % (slack + 1)
    lengths = lengths.at[donor].add(-passed).at[sink].add(passed)
    members = jnp.searchsorted(jnp.cumsum(lengths), jnp.arange(rows * top), side="right").astype(jnp.int32)
    table = members.reshape(top, rows).T
    table = table[jax.random.permutation(jax.random.fold_in(own, 1), rows)]
    turn = jax.random.randint(jax.random.fold_in(own, 2), (rows, 1), 0, top)
    return jnp.take_along_axis(table, (jnp.arange(top)[None, :] + turn) % top, axis=1)


def load_shares(number_of, total, reach, slope, full):
    loads = [(1 << 20) // math.isqrt(grade ** slope) + 1 for grade in range(1, number_of + 1)]
    largest = reach if full else min(reach, max(-(-total // number_of), total * loads[0] // sum(loads)))
    least = 1 if total - largest >= number_of - 1 else 0
    counts, surplus = [largest] + [least] * (number_of - 1), total - largest - least * (number_of - 1)
    while surplus > 0:
        movable = [i for i in range(1, number_of) if counts[i] < largest] or [i for i in range(1, number_of) if counts[i] < reach]
        pool, remaining = sum([loads[i] for i in movable]), surplus
        for i in movable:
            addition = min(reach - counts[i], max(1, remaining * loads[i] // pool), surplus)
            counts[i] = counts[i] + addition
            surplus = surplus - addition
    return np.array(counts)


def scatter_about(own_key, extent, deviation, bound, split=(), held_as=jnp.bfloat16):
    gain = block_levels(own_key, extent, split, -0.22, 0.18) if split else 1.0
    drawn = jax.random.normal(own_key, extent, jnp.float32) * deviation * gain
    return jnp.minimum(jnp.maximum(drawn, -bound), bound).astype(held_as)


def setup_inputs(seed: int = 0) -> dict:
    arg_keys = jax.random.split(jax.random.key(seed), 8)
    tokens = scatter_about(arg_keys[0], (TOKENS, D), 1.0, 6.0, ((0, 256),))
    out_grad = scatter_about(arg_keys[1], (TOKENS, D), 1.0, 6.0, ((0, 256),))
    gate_probs = jnp.clip(jnp.exp(math.log(0.59765625) - 2.4849066 * jax.random.uniform(arg_keys[2], (TOKENS, TOP), jnp.float32) ** block_levels(arg_keys[2], (TOKENS, TOP), ((0, 256),), -0.2, 0.2)), 0.049804688, 0.59765625).astype(jnp.bfloat16)
    expert_ids_keys = jax.random.split(jax.random.fold_in(arg_keys[3], 1), TOKENS // TOK_DEV)
    expert_ids_turns = jax.random.permutation(jax.random.fold_in(arg_keys[3], 3), TOKENS // TOK_DEV)
    expert_ids = jax.vmap(lambda own, number: deal_out(jax.random.fold_in(arg_keys[3], 2), own, number, TOK_DEV, EXPERTS, TOP, CAP, 2))(expert_ids_keys, expert_ids_turns).reshape((TOKENS, TOP))
    w_gate = scatter_about(arg_keys[4], (EXPERTS, D, H), D ** -0.5, 0.125, ((0, 64),))
    w_up = scatter_about(arg_keys[5], (EXPERTS, D, H), D ** -0.5, 0.125, ((0, 64),))
    w_down = scatter_about(arg_keys[6], (EXPERTS, H, D), H ** -0.5, 0.21875, ((0, 64),))
    return dict(tokens=tokens, out_grad=out_grad, gate_probs=gate_probs, expert_ids=expert_ids, w_gate=w_gate, w_up=w_up, w_down=w_down)


def expert_work(x_slots, dy_slots, prob_slots, gate_mat, up_mat, down_mat):
    gate_pre = jnp.dot(x_slots, gate_mat, preferred_element_type=jnp.float32)
    up_pre = jnp.dot(x_slots, up_mat, preferred_element_type=jnp.float32)
    sigmoid_gate = jax.nn.sigmoid(gate_pre)
    silu_gate = gate_pre * sigmoid_gate
    hidden_act = silu_gate * up_pre
    hidden = hidden_act.astype(jnp.bfloat16)
    grad_hidden = lax.dot_general(dy_slots, down_mat, (((1,), (1,)), ((), ())), preferred_element_type=jnp.float32)
    prob_grad = jnp.sum(hidden_act * grad_hidden, axis=1)
    scaled_hidden = prob_slots[:, None] * grad_hidden
    grad_gate = (scaled_hidden * up_pre * sigmoid_gate * (1.0 + gate_pre * (1.0 - sigmoid_gate))).astype(jnp.bfloat16)
    grad_up = (scaled_hidden * silu_gate).astype(jnp.bfloat16)
    scaled_dy = (prob_slots[:, None] * dy_slots.astype(jnp.float32)).astype(jnp.bfloat16)
    row_grad = lax.dot_general(grad_gate, gate_mat, (((1,), (1,)), ((), ())), preferred_element_type=jnp.float32)
    row_grad = row_grad + lax.dot_general(grad_up, up_mat, (((1,), (1,)), ((), ())), preferred_element_type=jnp.float32)
    return hidden, grad_gate, grad_up, scaled_dy, row_grad, prob_grad


def reference(tokens, out_grad, gate_probs, expert_ids, w_gate, w_up, w_down):
    devices = N_DP * N_EXPERT
    assigns = TOK_DEV * TOP
    block_ids = expert_ids.reshape(devices, assigns)
    onehot = (block_ids[:, :, None] == jnp.arange(EXPERTS, dtype=jnp.int32)[None, None, :]).astype(jnp.int32)
    slot_rank = jnp.sum((jnp.cumsum(onehot, axis=1) - onehot) * onehot, axis=2).astype(jnp.int32)
    slot_index = jnp.arange(devices, dtype=jnp.int32)[:, None] * CAP + slot_rank
    assign_index = jnp.arange(devices * assigns, dtype=jnp.int32).reshape(devices, assigns)
    tables = jnp.full((EXPERTS, devices * CAP), TOKENS * TOP, jnp.int32).at[block_ids, slot_index].set(assign_index)
    tokens_pad = jnp.concatenate([tokens, jnp.zeros((1, D), jnp.bfloat16)], axis=0)
    grad_pad = jnp.concatenate([out_grad, jnp.zeros((1, D), jnp.bfloat16)], axis=0)
    probs_pad = jnp.concatenate([gate_probs.reshape(-1).astype(jnp.float32), jnp.zeros((1,), jnp.float32)], axis=0)

    def step(carry, inputs):
        table, gate_mat, up_mat, down_mat = inputs
        token_row = (table // TOP).astype(jnp.int32)
        x_slots = tokens_pad[token_row]
        dy_slots = grad_pad[token_row]
        prob_slots = probs_pad[table]
        hidden, grad_gate, grad_up, scaled_dy, row_grad, prob_grad = expert_work(x_slots, dy_slots, prob_slots, gate_mat, up_mat, down_mat)
        gate_term = lax.dot_general(x_slots, grad_gate, (((0,), (0,)), ((), ())), preferred_element_type=jnp.float32)
        up_term = lax.dot_general(x_slots, grad_up, (((0,), (0,)), ((), ())), preferred_element_type=jnp.float32)
        down_term = lax.dot_general(hidden, scaled_dy, (((0,), (0,)), ((), ())), preferred_element_type=jnp.float32)
        tokens_acc = carry[0].at[token_row].add(row_grad)
        probs_acc = carry[1].at[table].add(prob_grad)
        return (tokens_acc, probs_acc), (gate_term.astype(jnp.bfloat16), up_term.astype(jnp.bfloat16), down_term.astype(jnp.bfloat16))

    start = (jnp.zeros((TOKENS + 1, D), jnp.float32), jnp.zeros((TOKENS * TOP + 1,), jnp.float32))
    finals, grads = lax.scan(step, start, (tables, w_gate, w_up, w_down))
    tokens_grad = finals[0][:TOKENS].astype(jnp.bfloat16)
    probs_grad = finals[1][:TOKENS * TOP].reshape(TOKENS, TOP)
    return tokens_grad, probs_grad, grads[0], grads[1], grads[2]
```

```python
import jax
import jax.numpy as jnp
from jax import lax
from jax.experimental import pallas as pl
from jax.experimental.pallas import tpu as pltpu
from jax.sharding import PartitionSpec as P

BF = jnp.bfloat16
F32 = jnp.float32
TOP = 4
TOK = 128
EXP = 64
MAIN = 8
ROWS = EXP * MAIN
ALL = ROWS + EXP
D = 2048
H = 768
SEG = D // MAIN
N_DP = 4
HS = H // N_DP
X_COLS = D + SEG
Y_COLS = D + SEG + 128


def dot(a, b):
    return jnp.dot(a, b, preferred_element_type=F32)


def dot_nt(a, b):
    return lax.dot_general(a, b, (((1,), (1,)), ((), ())), preferred_element_type=F32)


def dot_tn(a, b):
    return lax.dot_general(a, b, (((0,), (0,)), ((), ())), preferred_element_type=F32)


def iota(shape, axis):
    return lax.broadcasted_iota(jnp.int32, shape, axis)


def one(mask):
    return jnp.where(mask, 1.0, 0.0)


def slot_masks(ids):
    lane_e = iota((EXP, TOK), 0)
    picks = [ids[k : k + 1, :] == lane_e for k in range(TOP)]
    member = picks[0] | picks[1] | picks[2] | picks[3]
    before = one(iota((TOK, TOK), 0) < iota((TOK, TOK), 1)).astype(BF)
    rank = jnp.where(member, dot(one(member).astype(BF), before), 200.0)
    spread = one((iota((ROWS, EXP), 0) >> 3) == iota((ROWS, EXP), 1)).astype(BF)
    rank_rows = dot(spread, rank.astype(BF))
    return picks, spread, rank_rows


def spare_masks(rank_rows):
    sub = iota((ROWS, TOK), 0) & (MAIN - 1)
    ninth = rank_rows == float(MAIN)
    return [one(ninth & (sub == j)).astype(BF) for j in range(MAIN)]


def main_mask(rank_rows):
    sub = iota((ROWS, TOK), 0) & (MAIN - 1)
    return rank_rows == sub.astype(F32)


def pack_kernel(ids_ref, data_ref, probs_ref, out_ref, *, with_probs):
    picks, spread, rank_rows = slot_masks(ids_ref[...])
    main = one(main_mask(rank_rows))
    out_ref[:, :D] = dot(main.astype(BF), data_ref[...]).astype(BF)
    spare = jnp.concatenate(spare_masks(rank_rows), axis=1)
    parts = jnp.concatenate([data_ref[:, j * SEG : (j + 1) * SEG] for j in range(MAIN)], axis=0)
    out_ref[:, D : D + SEG] = dot(spare, parts).astype(BF)
    if with_probs:
        chosen = jnp.zeros((EXP, TOK), F32)
        for k in range(TOP):
            chosen = chosen + jnp.where(picks[k], probs_ref[k : k + 1, :], 0.0)
        prob_rows = dot(spread, chosen.astype(BF))
        p_main = jnp.sum(main * prob_rows, axis=1, keepdims=True)
        p_ninth = jnp.sum(
            jnp.where(rank_rows == float(MAIN), prob_rows, 0.0), axis=1, keepdims=True
        )
        lane = iota((ROWS, 128), 1)
        out_ref[:, D + SEG :] = jnp.where(
            lane == 0, p_main, jnp.where(lane == 1, p_ninth, 0.0)
        ).astype(BF)


def pack(ids, data, probs, with_probs):
    cols = Y_COLS if with_probs else X_COLS

    def kernel(ids_ref, data_ref, probs_ref, out_ref):
        pack_kernel(ids_ref, data_ref, probs_ref, out_ref, with_probs=with_probs)

    return pl.pallas_call(
        kernel,
        out_shape=jax.ShapeDtypeStruct((ROWS, cols), BF),
        name="pack_dy" if with_probs else "pack_x",
    )(ids, data, probs)


def unfold_mask():
    row = iota((ROWS, ROWS), 0)
    col = iota((ROWS, ROWS), 1)
    return one(col == (row & (EXP - 1)) * MAIN + (row >> 6)).astype(BF)


def fold_mask():
    row = iota((ROWS, ROWS), 0)
    col = iota((ROWS, ROWS), 1)
    return one(col == (row & (MAIN - 1)) * EXP + (row >> 3)).astype(BF)


def fill_rows(recv_ref, rows_ref):
    rows_ref[:ROWS, :] = recv_ref[:, :D]
    spare = dot(unfold_mask(), recv_ref[:, D : D + SEG]).astype(BF)
    for j in range(MAIN):
        rows_ref[ROWS:, j * SEG : (j + 1) * SEG] = spare[j * EXP : (j + 1) * EXP, :]


def forward_kernel(recv_ref, gate_ref, up_ref, slope_ref, silu_ref, act_ref, rows_ref):
    @pl.when(pl.program_id(0) == 0)
    def _():
        fill_rows(recv_ref, rows_ref)

    gate_pre = dot(rows_ref[...], gate_ref[...])
    up_pre = dot(rows_ref[...], up_ref[...])
    sig = jax.nn.sigmoid(gate_pre)
    silu = gate_pre * sig
    silu_ref[...] = silu
    act_ref[...] = silu * up_pre
    slope_ref[...] = up_pre * sig * (1.0 + gate_pre * (1.0 - sig))


def forward(recv_x, gate_mat, up_mat):
    full = pl.BlockSpec((ROWS, X_COLS), lambda j: (0, 0))
    weight = pl.BlockSpec((D, 256), lambda j: (0, j))
    out = pl.BlockSpec((ALL, 256), lambda j: (0, j))
    shape = jax.ShapeDtypeStruct((ALL, H), F32)
    return pl.pallas_call(
        forward_kernel,
        grid=(H // 256,),
        in_specs=[full, weight, weight],
        out_specs=[out, out, out],
        out_shape=[shape, shape, shape],
        scratch_shapes=[pltpu.VMEM((ALL, D), BF)],
        name="forward",
    )(recv_x, gate_mat, up_mat)


def grads_kernel(
    recv_ref, down_ref, slope_ref, silu_ref, act_ref,
    grad_ref, scaled_ref, tail_ref, rows_ref, prob_ref, sum_ref,
):
    step = pl.program_id(0)

    @pl.when(step == 0)
    def _():
        fill_rows(recv_ref, rows_ref)
        tail = recv_ref[:, D + SEG :]
        pick = one(iota((EXP, ROWS), 1) == iota((EXP, ROWS), 0) * MAIN).astype(BF)
        prob_ref[:ROWS, :] = tail[:, 0:1].astype(F32)
        prob_ref[ROWS:, :] = dot(pick, tail)[:, 1:2]
        scaled_ref[...] = (prob_ref[...] * rows_ref[...].astype(F32)).astype(BF)
        sum_ref[...] = jnp.zeros_like(sum_ref)

    grad_hidden = dot_nt(rows_ref[...], down_ref[...])
    sum_ref[...] += jnp.sum(act_ref[...] * grad_hidden, axis=1, keepdims=True)
    scaled = prob_ref[...] * grad_hidden
    grad_ref[0] = (scaled * slope_ref[...]).astype(BF)
    grad_ref[1] = (scaled * silu_ref[...]).astype(BF)

    @pl.when(step == H // 256 - 1)
    def _():
        total = sum_ref[...]
        high = total.astype(BF)
        low = (total - high.astype(F32)).astype(BF)
        lane = iota((EXP, 128), 1)
        ninth = jnp.where(
            lane == 2,
            high[ROWS:].astype(F32),
            jnp.where(lane == 3, low[ROWS:].astype(F32), 0.0),
        ).astype(BF)
        spread = one((iota((ROWS, EXP), 0) >> 3) == iota((ROWS, EXP), 1)).astype(BF)
        lane_rows = iota((ROWS, 128), 1)
        tail_ref[...] = jnp.where(
            lane_rows == 0,
            high[:ROWS].astype(F32),
            jnp.where(lane_rows == 1, low[:ROWS].astype(F32), dot(spread, ninth)),
        ).astype(BF)


def grads(recv_dy, down_mat, slope, silu, act):
    full = pl.BlockSpec((ROWS, Y_COLS), lambda j: (0, 0))
    block = pl.BlockSpec((ALL, 256), lambda j: (0, j))
    return pl.pallas_call(
        grads_kernel,
        grid=(H // 256,),
        in_specs=[full, pl.BlockSpec((256, D), lambda j: (j, 0)), block, block, block],
        out_specs=[
            pl.BlockSpec((2, ALL, 256), lambda j: (0, 0, j)),
            pl.BlockSpec((ALL, D), lambda j: (0, 0)),
            pl.BlockSpec((ROWS, 128), lambda j: (0, 0)),
        ],
        out_shape=[
            jax.ShapeDtypeStruct((2, ALL, H), BF),
            jax.ShapeDtypeStruct((ALL, D), BF),
            jax.ShapeDtypeStruct((ROWS, 128), BF),
        ],
        scratch_shapes=[
            pltpu.VMEM((ALL, D), BF),
            pltpu.VMEM((ALL, 1), F32),
            pltpu.VMEM((ALL, 1), F32),
        ],
        name="grads",
    )(recv_dy, down_mat, slope, silu, act)


def back_kernel(grad_ref, gate_ref, up_ref, tail_ref, out_ref, spare_ref):
    step = pl.program_id(0)
    row = dot_nt(grad_ref[0], gate_ref[...]) + dot_nt(grad_ref[1], up_ref[...])
    row = row.astype(BF)
    out_ref[:, pl.ds(pl.multiple_of(step * 512, 512), 512)] = row[:ROWS]
    for h in range(2):
        spare_ref[pl.ds(pl.multiple_of((2 * step + h) * EXP, EXP), EXP), :] = row[
            ROWS:, h * SEG : (h + 1) * SEG
        ]

    @pl.when(step == D // 512 - 1)
    def _():
        out_ref[:, D : D + SEG] = dot(fold_mask(), spare_ref[...]).astype(BF)
        out_ref[:, D + SEG :] = tail_ref[...]


def back(grad, gate_mat, up_mat, tail):
    weight = pl.BlockSpec((512, H), lambda j: (j, 0))
    return pl.pallas_call(
        back_kernel,
        grid=(D // 512,),
        in_specs=[
            pl.BlockSpec((2, ALL, H), lambda j: (0, 0, 0)),
            weight,
            weight,
            pl.BlockSpec((ROWS, 128), lambda j: (0, 0)),
        ],
        out_specs=pl.BlockSpec((ROWS, Y_COLS), lambda j: (0, 0)),
        out_shape=jax.ShapeDtypeStruct((ROWS, Y_COLS), BF),
        scratch_shapes=[pltpu.VMEM((ROWS, SEG), BF)],
        name="back",
    )(grad, gate_mat, up_mat, tail)


def slices_kernel(own_ref, grad_ref, *out_refs):
    own = own_ref[0]
    for t in range(N_DP):
        piece = jnp.concatenate(
            [grad_ref[0, :, t * HS : (t + 1) * HS], grad_ref[1, :, t * HS : (t + 1) * HS]],
            axis=1,
        )
        for d in range(N_DP):

            @pl.when((own + d) % N_DP == t)
            def _(piece=piece, d=d):
                out_refs[d][...] = piece


def slices(own, grad):
    shape = jax.ShapeDtypeStruct((ALL, 2 * HS), BF)
    vmem = pl.BlockSpec(memory_space=pltpu.VMEM)
    return pl.pallas_call(
        slices_kernel,
        in_specs=[pl.BlockSpec(memory_space=pltpu.SMEM), vmem],
        out_specs=[vmem] * N_DP,
        out_shape=[shape] * N_DP,
        name="slices",
    )(own, grad)


def down_kernel(own_ref, act_ref, scaled_ref, *out_refs):
    own = own_ref[0]
    hidden = act_ref[...].astype(BF)
    for t in range(N_DP):
        term = dot_tn(hidden[:, t * HS : (t + 1) * HS], scaled_ref[...]).astype(BF)
        for d in range(N_DP):

            @pl.when((own + d) % N_DP == t)
            def _(term=term, d=d):
                out_refs[d][...] = term


def down_terms(own, act, scaled):
    shape = jax.ShapeDtypeStruct((HS, D), BF)
    vmem = pl.BlockSpec(memory_space=pltpu.VMEM)
    return pl.pallas_call(
        down_kernel,
        in_specs=[pl.BlockSpec(memory_space=pltpu.SMEM), vmem, vmem],
        out_specs=[vmem] * N_DP,
        out_shape=[shape] * N_DP,
        name="down_terms",
    )(own, act, scaled)


def gate_up_kernel(*refs):
    x_refs, spare_refs, g_refs = refs[:N_DP], refs[N_DP : 2 * N_DP], refs[2 * N_DP : 3 * N_DP]
    gate_ref, up_ref, turned_ref = refs[3 * N_DP :]
    step = pl.program_id(0)

    @pl.when(step == 0)
    def _():
        for g in range(N_DP):
            turned = g_refs[g][...].astype(F32).T.astype(BF)
            turned_ref[:, g * ROWS : (g + 1) * ROWS] = turned[:, :ROWS]
            turned_ref[:, N_DP * ROWS + g * EXP : N_DP * ROWS + (g + 1) * EXP] = turned[:, ROWS:]

    pick = one(iota((EXP, ROWS), 1) == iota((EXP, ROWS), 0) * MAIN + step).astype(BF)
    spare = jnp.concatenate(
        [dot(pick, spare_refs[g][...]).astype(BF) for g in range(N_DP)], axis=0
    )
    total = dot(turned_ref[:, N_DP * ROWS :], spare)
    for g in range(N_DP):
        total = total + dot(turned_ref[:, g * ROWS : (g + 1) * ROWS], x_refs[g][...])
    total = total.T
    gate_ref[...] = total[:, :HS].astype(BF)
    up_ref[...] = total[:, HS:].astype(BF)


def gate_up_terms(xs, gs):
    main = pl.BlockSpec((ROWS, SEG), lambda j: (0, j))
    spare = pl.BlockSpec((ROWS, SEG), lambda j: (0, MAIN))
    grad = pl.BlockSpec((ALL, 2 * HS), lambda j: (0, 0))
    out = pl.BlockSpec((SEG, HS), lambda j: (j, 0))
    shape = jax.ShapeDtypeStruct((D, HS), BF)
    return pl.pallas_call(
        gate_up_kernel,
        grid=(MAIN,),
        in_specs=[main] * N_DP + [spare] * N_DP + [grad] * N_DP,
        out_specs=[out, out],
        out_shape=[shape, shape],
        scratch_shapes=[pltpu.VMEM((2 * HS, N_DP * ALL), BF)],
        name="gate_up_terms",
    )(*xs, *xs, *gs)


def combine_kernel(ids_ref, recv_ref, rows_ref, probs_ref):
    picks, _, rank_rows = slot_masks(ids_ref[...])
    main = one(main_mask(rank_rows))
    total = dot_tn(main.astype(BF), recv_ref[:, :D])
    spare = jnp.concatenate(spare_masks(rank_rows), axis=1)
    extra = dot_tn(spare, recv_ref[:, D : D + SEG])
    for j in range(MAIN):
        rows_ref[:, j * SEG : (j + 1) * SEG] = (
            total[:, j * SEG : (j + 1) * SEG] + extra[j * TOK : (j + 1) * TOK, :]
        ).astype(BF)
    tail = recv_ref[:, D + SEG :].astype(F32)
    v_main = tail[:, 0:1] + tail[:, 1:2]
    v_ninth = tail[:, 2:3] + tail[:, 3:4]
    ninth = one((rank_rows == float(MAIN)) & ((iota((ROWS, TOK), 0) & (MAIN - 1)) == 0))
    values = main * v_main + ninth * v_ninth
    owner = iota((ROWS, TOK), 0) >> 3
    for k in range(TOP):
        hit = ids_ref[k : k + 1, :] == owner
        probs_ref[k : k + 1, :] = jnp.sum(jnp.where(hit, values, 0.0), axis=0, keepdims=True)


def combine(ids, recv):
    return pl.pallas_call(
        combine_kernel,
        out_shape=[
            jax.ShapeDtypeStruct((TOK, D), BF),
            jax.ShapeDtypeStruct((TOP, TOK), F32),
        ],
        name="combine",
    )(ids, recv)


def exchange(flat):
    out = lax.all_to_all(
        flat.reshape(EXP, MAIN, flat.shape[1]), "expert", split_axis=0, concat_axis=0, tiled=True
    )
    return out.reshape(flat.shape)


def shift(value, by):
    return lax.ppermute(value, "dp", [(i, (i + by) % N_DP) for i in range(N_DP)])


def per_device(tokens, out_grad, gate_probs, expert_ids, w_gate, w_up, w_down):
    own = lax.axis_index("dp").astype(jnp.int32).reshape(1)
    ids = expert_ids.T
    probs = gate_probs.T.astype(F32)
    gate_mat, up_mat, down_mat = w_gate[0], w_up[0], w_down[0]
    recv_x = exchange(pack(ids, tokens, probs, False))
    recv_dy = exchange(pack(ids, out_grad, probs, True))
    xs = [recv_x] + [shift(recv_x, d) for d in range(1, N_DP)]
    slope, silu, act = forward(recv_x, gate_mat, up_mat)
    grad, scaled, tail = grads(recv_dy, down_mat, slope, silu, act)
    pieces = slices(own, grad)
    gs = [pieces[0]] + [shift(pieces[d], d) for d in range(1, N_DP)]
    back_rows = exchange(back(grad, gate_mat, up_mat, tail))
    terms = down_terms(own, act, scaled)
    downs = [terms[0]] + [shift(terms[d], d) for d in range(1, N_DP)]
    down_grad = downs[0].astype(F32)
    for d in range(1, N_DP):
        down_grad = down_grad + downs[d].astype(F32)
    gate_grad, up_grad = gate_up_terms(xs, gs)
    tokens_grad, probs_grad = combine(ids, back_rows)
    return (
        tokens_grad,
        probs_grad.T,
        gate_grad[None],
        up_grad[None],
        down_grad.astype(BF)[None],
    )


def solution(mesh):
    rows = P(("dp", "expert"), None)
    weights = P("expert", None, None)
    return jax.shard_map(
        per_device,
        mesh=mesh,
        in_specs=(rows, rows, rows, rows, weights, weights, weights),
        out_specs=(rows, rows, P("expert", None, "dp"), P("expert", None, "dp"), P("expert", "dp", None)),
        check_vma=False,
    )
```

```python
import jax
import jax.numpy as jnp
from jax import lax
from jax.experimental import pallas as pl
from jax.experimental.pallas import tpu as pltpu
from jax.sharding import PartitionSpec as P


BF = jnp.bfloat16
F32 = jnp.float32
TOP = 4
TOK = 128
EXP = 64
MAIN = 8
ROWS = EXP * MAIN
ALL = ROWS + EXP
D = 2048
H = 768
SEG = D // MAIN
N_DP = 4
HS = H // N_DP
X_COLS = D + SEG
Y_COLS = D + SEG + 128


def dot(a, b):
    return jnp.dot(a, b, preferred_element_type=F32)


def dot_nt(a, b):
    return lax.dot_general(a, b, (((1,), (1,)), ((), ())), preferred_element_type=F32)


def dot_tn(a, b):
    return lax.dot_general(a, b, (((0,), (0,)), ((), ())), preferred_element_type=F32)


def iota(shape, axis):
    return lax.broadcasted_iota(jnp.int32, shape, axis)


def one(mask):
    return jnp.where(mask, 1.0, 0.0)


def slot_masks(ids):
    lane_e = iota((EXP, TOK), 0)
    picks = [ids[k : k + 1, :] == lane_e for k in range(TOP)]
    member = picks[0] | picks[1] | picks[2] | picks[3]
    before = one(iota((TOK, TOK), 0) < iota((TOK, TOK), 1)).astype(BF)
    rank = jnp.where(member, dot(one(member).astype(BF), before), 200.0)
    spread = one((iota((ROWS, EXP), 0) >> 3) == iota((ROWS, EXP), 1)).astype(BF)
    rank_rows = dot(spread, rank.astype(BF))
    return picks, spread, rank_rows


def spare_masks(rank_rows):
    sub = iota((ROWS, TOK), 0) & (MAIN - 1)
    ninth = rank_rows == float(MAIN)
    return [one(ninth & (sub == j)).astype(BF) for j in range(MAIN)]


def main_mask(rank_rows):
    sub = iota((ROWS, TOK), 0) & (MAIN - 1)
    return rank_rows == sub.astype(F32)


def pack_rows(ids_ref, data_ref, out_ref):
    picks, spread, rank_rows = slot_masks(ids_ref[...])
    main = one(main_mask(rank_rows))
    out_ref[:, :D] = dot(main.astype(BF), data_ref[...]).astype(BF)
    spare = jnp.concatenate(spare_masks(rank_rows), axis=1)
    parts = jnp.concatenate([data_ref[:, j * SEG : (j + 1) * SEG] for j in range(MAIN)], axis=0)
    out_ref[:, D : D + SEG] = dot(spare, parts).astype(BF)
    return picks, spread, rank_rows, main


def pack_x_kernel(ids_ref, data_ref, out_ref):
    pack_rows(ids_ref, data_ref, out_ref)


def pack_dy_kernel(ids_ref, data_ref, probs_ref, out_ref):
    picks, spread, rank_rows, main = pack_rows(ids_ref, data_ref, out_ref)
    probs = probs_ref[...].astype(F32)
    chosen = jnp.zeros((EXP, TOK), F32)
    for k in range(TOP):
        chosen = chosen + jnp.where(picks[k], probs[k : k + 1, :], 0.0)
    prob_rows = dot(spread, chosen.astype(BF))
    p_main = jnp.sum(main * prob_rows, axis=1, keepdims=True)
    p_ninth = jnp.sum(jnp.where(rank_rows == float(MAIN), prob_rows, 0.0), axis=1, keepdims=True)
    lane = iota((ROWS, 128), 1)
    out_ref[:, D + SEG :] = jnp.where(
        lane == 0, p_main, jnp.where(lane == 1, p_ninth, 0.0)
    ).astype(BF)


def pack_x(ids, data):
    return pl.pallas_call(
        pack_x_kernel, out_shape=jax.ShapeDtypeStruct((ROWS, X_COLS), BF), name="pack_x"
    )(ids, data)


def pack_dy(ids, data, probs):
    return pl.pallas_call(
        pack_dy_kernel, out_shape=jax.ShapeDtypeStruct((ROWS, Y_COLS), BF), name="pack_dy"
    )(ids, data, probs)


def unfold_mask():
    row = iota((ROWS, ROWS), 0)
    col = iota((ROWS, ROWS), 1)
    return one(col == (row & (EXP - 1)) * MAIN + (row >> 6)).astype(BF)


def fold_mask():
    row = iota((ROWS, ROWS), 0)
    col = iota((ROWS, ROWS), 1)
    return one(col == (row & (MAIN - 1)) * EXP + (row >> 3)).astype(BF)


def fill_rows(recv_ref, rows_ref):
    rows_ref[:ROWS, :] = recv_ref[:, :D]
    spare = dot(unfold_mask(), recv_ref[:, D : D + SEG]).astype(BF)
    for j in range(MAIN):
        rows_ref[ROWS:, j * SEG : (j + 1) * SEG] = spare[j * EXP : (j + 1) * EXP, :]


def forward_kernel(recv_ref, gate_ref, up_ref, slope_ref, silu_ref, act_ref, rows_ref):
    @pl.when(pl.program_id(0) == 0)
    def _():
        fill_rows(recv_ref, rows_ref)

    gate_pre = dot(rows_ref[...], gate_ref[...])
    up_pre = dot(rows_ref[...], up_ref[...])
    sig = jax.nn.sigmoid(gate_pre)
    silu = gate_pre * sig
    silu_ref[...] = silu
    act_ref[...] = silu * up_pre
    slope_ref[...] = up_pre * sig * (1.0 + gate_pre * (1.0 - sig))


def forward(recv_x, gate_mat, up_mat):
    full = pl.BlockSpec((ROWS, X_COLS), lambda j: (0, 0))
    weight = pl.BlockSpec((D, 256), lambda j: (0, j))
    out = pl.BlockSpec((ALL, 256), lambda j: (0, j))
    shape = jax.ShapeDtypeStruct((ALL, H), F32)
    return pl.pallas_call(
        forward_kernel,
        grid=(H // 256,),
        in_specs=[full, weight, weight],
        out_specs=[out, out, out],
        out_shape=[shape, shape, shape],
        scratch_shapes=[pltpu.VMEM((ALL, D), BF)],
        name="forward",
    )(recv_x, gate_mat, up_mat)


H_STEPS = H // 256
D_STEPS = D // 512


def rows_kernel(
    recv_ref, down_ref, slope_ref, silu_ref, act_ref, gate_ref, up_ref,
    grad_ref, prob_out_ref, back_ref, rows_ref, prob_ref, sum_ref, spare_ref,
):
    step = pl.program_id(0)

    @pl.when(step == 0)
    def _():
        fill_rows(recv_ref, rows_ref)
        tail = recv_ref[:, D + SEG :]
        pick = one(iota((EXP, ROWS), 1) == iota((EXP, ROWS), 0) * MAIN).astype(BF)
        prob_ref[:ROWS, :] = tail[:, 0:1].astype(F32)
        prob_ref[ROWS:, :] = dot(pick, tail)[:, 1:2]
        sum_ref[...] = jnp.zeros_like(sum_ref)

    for h in range(H_STEPS):

        @pl.when(step == h)
        def _(h=h):
            grad_hidden = dot_nt(rows_ref[...], down_ref[...])
            sum_ref[...] += jnp.sum(act_ref[...] * grad_hidden, axis=1, keepdims=True)
            scaled = prob_ref[...] * grad_hidden
            grad_ref[0, :, h * 256 : (h + 1) * 256] = (scaled * slope_ref[...]).astype(BF)
            grad_ref[1, :, h * 256 : (h + 1) * 256] = (scaled * silu_ref[...]).astype(BF)

    for q in range(D_STEPS):

        @pl.when(step == H_STEPS + q)
        def _(q=q):
            row = dot_nt(grad_ref[0], gate_ref[...]) + dot_nt(grad_ref[1], up_ref[...])
            row = row.astype(BF)
            back_ref[:, q * 512 : (q + 1) * 512] = row[:ROWS]
            for h in range(2):
                spare_ref[(2 * q + h) * EXP : (2 * q + h + 1) * EXP, :] = row[
                    ROWS:, h * SEG : (h + 1) * SEG
                ]

    @pl.when(step == H_STEPS + D_STEPS - 1)
    def _():
        back_ref[:, D : D + SEG] = dot(fold_mask(), spare_ref[...]).astype(BF)
        total = sum_ref[...]
        high = total.astype(BF)
        low = (total - high.astype(F32)).astype(BF)
        lane = iota((EXP, 128), 1)
        ninth = jnp.where(
            lane == 2,
            high[ROWS:].astype(F32),
            jnp.where(lane == 3, low[ROWS:].astype(F32), 0.0),
        ).astype(BF)
        spread = one((iota((ROWS, EXP), 0) >> 3) == iota((ROWS, EXP), 1)).astype(BF)
        lane_rows = iota((ROWS, 128), 1)
        back_ref[:, D + SEG :] = jnp.where(
            lane_rows == 0,
            high[:ROWS].astype(F32),
            jnp.where(lane_rows == 1, low[:ROWS].astype(F32), dot(spread, ninth)),
        ).astype(BF)
        prob_out_ref[...] = jnp.broadcast_to(prob_ref[...], (ALL, 128))


def rows_pass(recv_dy, down_mat, slope, silu, act, gate_mat, up_mat):
    last_h = H_STEPS - 1
    full = pl.BlockSpec((ROWS, Y_COLS), lambda j: (0, 0))
    block = pl.BlockSpec((ALL, 256), lambda j: (0, jnp.minimum(j, last_h)))
    weight = pl.BlockSpec((512, H), lambda j: (jnp.maximum(j - H_STEPS, 0), 0))
    return pl.pallas_call(
        rows_kernel,
        grid=(H_STEPS + D_STEPS,),
        in_specs=[
            full,
            pl.BlockSpec((256, D), lambda j: (jnp.minimum(j, last_h), 0)),
            block, block, block, weight, weight,
        ],
        out_specs=[
            pl.BlockSpec((2, ALL, H), lambda j: (0, 0, 0)),
            pl.BlockSpec((ALL, 128), lambda j: (0, 0)),
            full,
        ],
        out_shape=[
            jax.ShapeDtypeStruct((2, ALL, H), BF),
            jax.ShapeDtypeStruct((ALL, 128), F32),
            jax.ShapeDtypeStruct((ROWS, Y_COLS), BF),
        ],
        scratch_shapes=[
            pltpu.VMEM((ALL, D), BF),
            pltpu.VMEM((ALL, 1), F32),
            pltpu.VMEM((ALL, 1), F32),
            pltpu.VMEM((ROWS, SEG), BF),
        ],
        name="rows_pass",
    )(recv_dy, down_mat, slope, silu, act, gate_mat, up_mat)


def slices_kernel(own_ref, grad_ref, *out_refs):
    own = own_ref[0]
    for t in range(N_DP):
        piece = jnp.concatenate(
            [grad_ref[0, :, t * HS : (t + 1) * HS], grad_ref[1, :, t * HS : (t + 1) * HS]],
            axis=1,
        )
        for d in range(N_DP):

            @pl.when((own + d) % N_DP == t)
            def _(piece=piece, d=d):
                out_refs[d][...] = piece


def slices(own, grad):
    shape = jax.ShapeDtypeStruct((ALL, 2 * HS), BF)
    vmem = pl.BlockSpec(memory_space=pltpu.VMEM)
    return pl.pallas_call(
        slices_kernel,
        in_specs=[pl.BlockSpec(memory_space=pltpu.SMEM), vmem],
        out_specs=[vmem] * N_DP,
        out_shape=[shape] * N_DP,
        name="slices",
    )(own, grad)


def down_kernel(own_ref, act_ref, recv_ref, prob_ref, *refs):
    out_refs, rows_ref = refs[:N_DP], refs[N_DP]
    own = own_ref[0]
    fill_rows(recv_ref, rows_ref)
    scaled = (prob_ref[:, 0:1] * rows_ref[...].astype(F32)).astype(BF)
    hidden = act_ref[...].astype(BF)
    for t in range(N_DP):
        term = dot_tn(hidden[:, t * HS : (t + 1) * HS], scaled).astype(BF)
        for d in range(N_DP):

            @pl.when((own + d) % N_DP == t)
            def _(term=term, d=d):
                out_refs[d][...] = term


def down_terms(own, act, recv_dy, prob):
    shape = jax.ShapeDtypeStruct((HS, D), BF)
    vmem = pl.BlockSpec(memory_space=pltpu.VMEM)
    return pl.pallas_call(
        down_kernel,
        in_specs=[pl.BlockSpec(memory_space=pltpu.SMEM), vmem, vmem, vmem],
        out_specs=[vmem] * N_DP,
        out_shape=[shape] * N_DP,
        scratch_shapes=[pltpu.VMEM((ALL, D), BF)],
        name="down_terms",
    )(own, act, recv_dy, prob)


HALF = ROWS // 2
X_PARTS = (1, 2, 2, 2)


def gate_up_kernel(*refs):
    n_x = sum(X_PARTS)
    x_refs, spare_refs, g_refs = refs[:n_x], refs[n_x : 2 * n_x], refs[2 * n_x : 2 * n_x + N_DP]
    gate_ref, up_ref, turned_ref = refs[2 * n_x + N_DP :]
    step = pl.program_id(0)

    @pl.when(step == 0)
    def _():
        for g in range(N_DP):
            turned = g_refs[g][...].astype(F32).T.astype(BF)
            turned_ref[:, g * ROWS : (g + 1) * ROWS] = turned[:, :ROWS]
            turned_ref[:, N_DP * ROWS + g * EXP : N_DP * ROWS + (g + 1) * EXP] = turned[:, ROWS:]

    spares = []
    total = jnp.zeros((2 * HS, SEG), F32)
    at = 0
    for x_ref, spare_ref in zip(x_refs, spare_refs):
        n = x_ref.shape[0]
        pick = one(iota((n // MAIN, n), 1) == iota((n // MAIN, n), 0) * MAIN + step).astype(BF)
        spares.append(dot(pick, spare_ref[...]).astype(BF))
        total = total + dot(turned_ref[:, at : at + n], x_ref[...])
        at += n
    total = total + dot(turned_ref[:, at:], jnp.concatenate(spares, axis=0))
    gate_ref[...] = total[:HS].astype(BF)
    up_ref[...] = total[HS:].astype(BF)


def gate_up_terms(xs, gs):
    mains = [pl.BlockSpec((x.shape[0], SEG), lambda j: (0, j)) for x in xs]
    spares = [pl.BlockSpec((x.shape[0], SEG), lambda j: (0, MAIN)) for x in xs]
    grad = pl.BlockSpec((ALL, 2 * HS), lambda j: (0, 0))
    out = pl.BlockSpec((HS, SEG), lambda j: (0, j))
    shape = jax.ShapeDtypeStruct((HS, D), BF)
    return pl.pallas_call(
        gate_up_kernel,
        grid=(MAIN,),
        in_specs=mains + spares + [grad] * N_DP,
        out_specs=[out, out],
        out_shape=[shape, shape],
        scratch_shapes=[pltpu.VMEM((2 * HS, N_DP * ALL), BF)],
        name="gate_up_terms",
    )(*xs, *xs, *gs)


def combine_kernel(ids_ref, recv_ref, rows_ref, probs_ref):
    _, _, rank_rows = slot_masks(ids_ref[...])
    main = one(main_mask(rank_rows))
    total = dot_tn(main.astype(BF), recv_ref[:, :D])
    spare = jnp.concatenate(spare_masks(rank_rows), axis=1)
    extra = dot_tn(spare, recv_ref[:, D : D + SEG])
    for j in range(MAIN):
        rows_ref[:, j * SEG : (j + 1) * SEG] = (
            total[:, j * SEG : (j + 1) * SEG] + extra[j * TOK : (j + 1) * TOK, :]
        ).astype(BF)
    tail = recv_ref[:, D + SEG :].astype(F32)
    v_main = tail[:, 0:1] + tail[:, 1:2]
    v_ninth = tail[:, 2:3] + tail[:, 3:4]
    ninth = one((rank_rows == float(MAIN)) & ((iota((ROWS, TOK), 0) & (MAIN - 1)) == 0))
    values = main * v_main + ninth * v_ninth
    owner = iota((ROWS, TOK), 0) >> 3
    for k in range(TOP):
        hit = ids_ref[k : k + 1, :] == owner
        probs_ref[k : k + 1, :] = jnp.sum(jnp.where(hit, values, 0.0), axis=0, keepdims=True)


def combine(ids, recv):
    return pl.pallas_call(
        combine_kernel,
        out_shape=[
            jax.ShapeDtypeStruct((TOK, D), BF),
            jax.ShapeDtypeStruct((TOP, TOK), F32),
        ],
        name="combine",
    )(ids, recv)


def exchange(flat):
    out = lax.all_to_all(
        flat.reshape(EXP, MAIN, flat.shape[1]), "expert", split_axis=0, concat_axis=0, tiled=True
    )
    return out.reshape(flat.shape)


def shift(value, by):
    return lax.ppermute(value, "dp", [(i, (i + by) % N_DP) for i in range(N_DP)])


def gather_rows(recv):
    top, low = recv[:HALF], recv[HALF:]
    prev_top = shift(top, 1)
    next_low = shift(low, 3)
    prev_low = shift(low, 1)
    next_top = shift(top, 3)
    far_top = shift(prev_top, 1)
    far_low = shift(next_low, 3)
    return [recv, prev_top, prev_low, far_top, far_low, next_top, next_low]


def per_device(tokens, out_grad, gate_probs, expert_ids, w_gate, w_up, w_down):
    own = lax.axis_index("dp").astype(jnp.int32).reshape(1)
    ids = expert_ids.T
    gate_mat, up_mat, down_mat = w_gate[0], w_up[0], w_down[0]
    recv_x = exchange(pack_x(ids, tokens))
    recv_dy = exchange(pack_dy(ids, out_grad, gate_probs.T))
    xs = gather_rows(recv_x)
    slope, silu, act = forward(recv_x, gate_mat, up_mat)
    grad, prob, back = rows_pass(recv_dy, down_mat, slope, silu, act, gate_mat, up_mat)
    back_rows = exchange(back)
    pieces = slices(own, grad)
    gs = [pieces[0]] + [shift(pieces[d], d) for d in range(1, N_DP)]
    terms = down_terms(own, act, recv_dy, prob)
    downs = [terms[0]] + [shift(terms[d], d) for d in range(1, N_DP)]
    gate_grad, up_grad = gate_up_terms(xs, gs)
    down_grad = downs[0].astype(F32)
    for d in range(1, N_DP):
        down_grad = down_grad + downs[d].astype(F32)
    tokens_grad, probs_grad = combine(ids, back_rows)
    return (
        tokens_grad,
        probs_grad.T,
        gate_grad.T[None],
        up_grad.T[None],
        down_grad.astype(BF)[None],
    )


def solution(mesh):
    rows = P(("dp", "expert"), None)
    weights = P("expert", None, None)
    return jax.shard_map(
        per_device,
        mesh=mesh,
        in_specs=(rows, rows, rows, rows, weights, weights, weights),
        out_specs=(rows, rows, P("expert", None, "dp"), P("expert", None, "dp"), P("expert", "dp", None)),
        check_vma=False,
    )
```

```python
import jax
import jax.numpy as jnp
from jax import lax
from jax.experimental import pallas as pl
from jax.experimental.pallas import tpu as pltpu
from jax.sharding import PartitionSpec as P


BF = jnp.bfloat16
F32 = jnp.float32
TOP = 4
TOK = 128
EXP = 64
MAIN = 8
ROWS = EXP * MAIN
ALL = ROWS + EXP
D = 2048
H = 768
SEG = D // MAIN
N_DP = 4
HS = H // N_DP
X_COLS = D + SEG
Y_COLS = D + SEG + 128


def dot(a, b):
    return jnp.dot(a, b, preferred_element_type=F32)


def dot_nt(a, b):
    return lax.dot_general(a, b, (((1,), (1,)), ((), ())), preferred_element_type=F32)


def iota(shape, axis):
    return lax.broadcasted_iota(jnp.int32, shape, axis)


def one(mask):
    return jnp.where(mask, 1.0, 0.0)


PACK_STEPS = 2
PACK = ROWS // PACK_STEPS


def pack_rows(ids_ref, data_ref, out_ref, rank_ref, probs_ref=None, chosen_ref=None):
    step = pl.program_id(0)

    @pl.when(step == 0)
    def _():
        ids = ids_ref[...]
        lane_e = iota((EXP, TOK), 0)
        picks = [ids[k : k + 1, :] == lane_e for k in range(TOP)]
        member = picks[0] | picks[1] | picks[2] | picks[3]
        before = one(iota((TOK, TOK), 0) < iota((TOK, TOK), 1)).astype(BF)
        rank_ref[...] = jnp.where(member, dot(one(member).astype(BF), before), 200.0).astype(BF)
        if probs_ref is not None:
            probs = probs_ref[...].astype(F32)
            chosen = jnp.zeros((EXP, TOK), F32)
            for k in range(TOP):
                chosen = chosen + jnp.where(picks[k], probs[k : k + 1, :], 0.0)
            chosen_ref[...] = chosen.astype(BF)

    expert = (iota((PACK, EXP), 0) >> 3) + step * (PACK // MAIN)
    spread = one(expert == iota((PACK, EXP), 1)).astype(BF)
    rank_rows = dot(spread, rank_ref[...])
    sub = iota((PACK, TOK), 0) & (MAIN - 1)
    main = rank_rows == sub.astype(F32)
    ninth = rank_rows == float(MAIN)
    spare = jnp.concatenate([one(ninth & (sub == j)).astype(BF) for j in range(MAIN)], axis=1)
    parts = jnp.concatenate([data_ref[:, j * SEG : (j + 1) * SEG] for j in range(MAIN)], axis=0)
    rows = dot(one(main).astype(BF), data_ref[...])
    extra = dot(spare, parts)
    if probs_ref is not None:
        prob_rows = dot(spread, chosen_ref[...])
        rows = rows * jnp.sum(jnp.where(main, prob_rows, 0.0), axis=1, keepdims=True)
        extra = extra * jnp.sum(jnp.where(ninth, prob_rows, 0.0), axis=1, keepdims=True)
    out_ref[:, :D] = rows.astype(BF)
    out_ref[:, D:] = extra.astype(BF)


def pack_x_kernel(ids_ref, data_ref, out_ref, rank_ref):
    pack_rows(ids_ref, data_ref, out_ref, rank_ref)


def pack_dy_kernel(ids_ref, data_ref, probs_ref, out_ref, rank_ref, chosen_ref):
    pack_rows(ids_ref, data_ref, out_ref, rank_ref, probs_ref, chosen_ref)


def pack(kernel, *args):
    return pl.pallas_call(
        kernel,
        grid=(PACK_STEPS,),
        in_specs=[pl.BlockSpec(x.shape, lambda j: (0, 0)) for x in args],
        out_specs=pl.BlockSpec((PACK, X_COLS), lambda j: (j, 0)),
        out_shape=jax.ShapeDtypeStruct((ROWS, X_COLS), BF),
        scratch_shapes=[pltpu.VMEM((EXP, TOK), BF)] * (len(args) - 1),
    )(*args)


def unfold_mask():
    row = iota((ROWS, ROWS), 0)
    col = iota((ROWS, ROWS), 1)
    return one(col == (row & (EXP - 1)) * MAIN + (row >> 6)).astype(BF)


def fold_mask():
    row = iota((ROWS, ROWS), 0)
    col = iota((ROWS, ROWS), 1)
    return one(col == (row & (MAIN - 1)) * EXP + (row >> 3)).astype(BF)


def fill_rows(recv_ref, rows_ref):
    rows_ref[:ROWS, :] = recv_ref[:, :D]
    spare = dot(unfold_mask(), recv_ref[:, D : D + SEG]).astype(BF)
    for j in range(MAIN):
        rows_ref[ROWS:, j * SEG : (j + 1) * SEG] = spare[j * EXP : (j + 1) * EXP, :]


def forward_kernel(
    recv_ref, gate_ref, up_ref, slope_ref, silu_ref, act_ref, turned_ref, rows_ref
):
    @pl.when(pl.program_id(0) == 0)
    def _():
        fill_rows(recv_ref, rows_ref)

    gate_pre = dot(rows_ref[...], gate_ref[...])
    up_pre = dot(rows_ref[...], up_ref[...])
    sig = jax.nn.sigmoid(gate_pre)
    silu = gate_pre * sig
    silu_ref[...] = silu
    act = silu * up_pre
    act_ref[...] = act
    turned_ref[...] = act.T.astype(BF)
    slope_ref[...] = up_pre * sig * (1.0 + gate_pre * (1.0 - sig))


def forward(recv_x, gate_mat, up_mat):
    full = pl.BlockSpec((ROWS, X_COLS), lambda j: (0, 0))
    weight = pl.BlockSpec((D, 256), lambda j: (0, j))
    out = pl.BlockSpec((ALL, 256), lambda j: (0, j))
    shape = jax.ShapeDtypeStruct((ALL, H), F32)
    return pl.pallas_call(
        forward_kernel,
        grid=(H // 256,),
        in_specs=[full, weight, weight],
        out_specs=[out, out, out, pl.BlockSpec((256, ALL), lambda j: (j, 0))],
        out_shape=[shape, shape, shape, jax.ShapeDtypeStruct((H, ALL), BF)],
        scratch_shapes=[pltpu.VMEM((ALL, D), BF)],
        name="forward",
    )(recv_x, gate_mat, up_mat)


def fill_spare(rows_ref, spare_ref):
    spare = dot(unfold_mask(), spare_ref[...]).astype(BF)
    for j in range(MAIN):
        rows_ref[ROWS:, j * SEG : (j + 1) * SEG] = spare[j * EXP : (j + 1) * EXP, :]


def start(source, target, sem):
    copy = pltpu.make_async_copy(source, target, sem)
    copy.start()
    return copy


def cols(ref, first, count):
    return ref.at[:, pl.ds(first, count)]


def rows_kernel(
    own_ref, recv_ref, down_ref, slope_ref, silu_ref, act_ref, gate_ref, up_ref,
    back_ref, piece0_ref, piece1_ref, piece2_ref, piece3_ref,
    rows_v, extra_v, down_v, slope_v, silu_v, act_v, weight_v, grad_v, piece_v, back_v, spare_v,
    sem_in, sem_out,
):
    pieces = [piece0_ref, piece1_ref, piece2_ref, piece3_ref]
    first = [
        start(cols(recv_ref, 0, D), rows_v.at[pl.ds(0, ROWS)], sem_in.at[0]),
        start(cols(recv_ref, D, SEG), extra_v, sem_in.at[1]),
    ]
    down_in = start(down_ref, down_v, sem_in.at[2])
    terms_in = [
        start(act_ref, act_v, sem_in.at[3]),
        start(slope_ref, slope_v, sem_in.at[4]),
        start(silu_ref, silu_v, sem_in.at[5]),
    ]
    for copy in first:
        copy.wait()
    weights_in = [
        start(gate_ref, cols(weight_v, 0, H), sem_in.at[6]),
        start(up_ref, cols(weight_v, H, H), sem_in.at[7]),
    ]
    fill_spare(rows_v, extra_v)
    down_in.wait()
    grad_hidden = dot_nt(rows_v[...], down_v[...])
    for copy in terms_in:
        copy.wait()
    total = jnp.sum(act_v[...] * grad_hidden, axis=1, keepdims=True)
    grad_v[:, :H] = (grad_hidden * slope_v[...]).astype(BF)
    grad_v[:, H:] = (grad_hidden * silu_v[...]).astype(BF)
    for copy in weights_in:
        copy.wait()
    outs = []
    own = own_ref[0]
    for q in range(2):
        n = D // 2
        row = dot_nt(grad_v[...], weight_v[q * n : (q + 1) * n, :]).astype(BF)
        back_v[:, q * n : (q + 1) * n] = row[:ROWS]
        for j in range(MAIN // 2):
            at = (q * (MAIN // 2) + j) * EXP
            spare_v[at : at + EXP, :] = row[ROWS:, j * SEG : (j + 1) * SEG]
        outs.append(start(cols(back_v, q * n, n), cols(back_ref, q * n, n), sem_out.at[q]))
        if q == 0:
            for t in range(N_DP):
                piece_v[t, :, :HS] = grad_v[:, t * HS : (t + 1) * HS]
                piece_v[t, :, HS:] = grad_v[:, H + t * HS : H + (t + 1) * HS]
            for d in range(N_DP):
                t = lax.rem(own + d, N_DP)
                outs.append(start(piece_v.at[t], pieces[d], sem_out.at[2 + d]))
    back_v[:, D : D + SEG] = dot(fold_mask(), spare_v[...]).astype(BF)
    high = total.astype(BF)
    low = (total - high.astype(F32)).astype(BF)
    lane = iota((EXP, 128), 1)
    ninth = jnp.where(
        lane == 2,
        high[ROWS:].astype(F32),
        jnp.where(lane == 3, low[ROWS:].astype(F32), 0.0),
    ).astype(BF)
    spread = one((iota((ROWS, EXP), 0) >> 3) == iota((ROWS, EXP), 1)).astype(BF)
    lane_rows = iota((ROWS, 128), 1)
    back_v[:, D + SEG :] = jnp.where(
        lane_rows == 0,
        high[:ROWS].astype(F32),
        jnp.where(lane_rows == 1, low[:ROWS].astype(F32), dot(spread, ninth)),
    ).astype(BF)
    outs.append(start(cols(back_v, D, SEG + 128), cols(back_ref, D, SEG + 128), sem_out.at[6]))
    for copy in outs:
        copy.wait()


def rows_pass(own, recv_dy, down_mat, slope, silu, act, gate_mat, up_mat):
    hbm = pl.BlockSpec(memory_space=pltpu.HBM)
    piece = jax.ShapeDtypeStruct((ALL, 2 * HS), BF)
    return pl.pallas_call(
        rows_kernel,
        in_specs=[pl.BlockSpec(memory_space=pltpu.SMEM)] + [hbm] * 7,
        out_specs=[hbm] * (1 + N_DP),
        out_shape=[jax.ShapeDtypeStruct((ROWS, Y_COLS), BF)] + [piece] * N_DP,
        scratch_shapes=[
            pltpu.VMEM((ALL, D), BF),
            pltpu.VMEM((ROWS, SEG), BF),
            pltpu.VMEM((H, D), BF),
            pltpu.VMEM((ALL, H), F32),
            pltpu.VMEM((ALL, H), F32),
            pltpu.VMEM((ALL, H), F32),
            pltpu.VMEM((D, 2 * H), BF),
            pltpu.VMEM((ALL, 2 * H), BF),
            pltpu.VMEM((N_DP, ALL, 2 * HS), BF),
            pltpu.VMEM((ROWS, Y_COLS), BF),
            pltpu.VMEM((ROWS, SEG), BF),
            pltpu.SemaphoreType.DMA((8,)),
            pltpu.SemaphoreType.DMA((7,)),
        ],
        name="rows_pass",
    )(own, recv_dy, down_mat, slope, silu, act, gate_mat, up_mat)


def down_kernel(
    own_ref, turned_ref, recv_ref, out0_ref, out1_ref, out2_ref, out3_ref,
    rows_v, extra_v, turned_v, out_v, sem_in, sem_out,
):
    outs_ref = [out0_ref, out1_ref, out2_ref, out3_ref]
    ins = [
        start(cols(recv_ref, D, SEG), extra_v, sem_in.at[1]),
        start(cols(recv_ref, 0, D), rows_v.at[pl.ds(0, ROWS)], sem_in.at[0]),
        start(turned_ref, turned_v, sem_in.at[2]),
    ]
    ins[0].wait()
    fill_spare(rows_v, extra_v)
    ins[1].wait()
    ins[2].wait()
    outs = []
    for n in range(N_DP):
        d = (n + 1) % N_DP
        at = pl.multiple_of(lax.rem(own_ref[0] + d, N_DP) * HS, HS)
        out_v[d] = dot(turned_v[pl.ds(at, HS), :], rows_v[...]).astype(BF)
        outs.append(start(out_v.at[d], outs_ref[d], sem_out.at[d]))
    for copy in outs:
        copy.wait()


def down_terms(own, turned, recv_dy):
    hbm = pl.BlockSpec(memory_space=pltpu.HBM)
    return pl.pallas_call(
        down_kernel,
        in_specs=[pl.BlockSpec(memory_space=pltpu.SMEM), hbm, hbm],
        out_specs=[hbm] * N_DP,
        out_shape=[jax.ShapeDtypeStruct((HS, D), BF)] * N_DP,
        scratch_shapes=[
            pltpu.VMEM((ALL, D), BF),
            pltpu.VMEM((ROWS, SEG), BF),
            pltpu.VMEM((H, ALL), BF),
            pltpu.VMEM((N_DP, HS, D), BF),
            pltpu.SemaphoreType.DMA((3,)),
            pltpu.SemaphoreType.DMA((N_DP,)),
        ],
        name="down_terms",
    )(own, turned, recv_dy)


HALF = ROWS // 2
X_PARTS = (1, 2, 2, 2)


def gate_up_kernel(*refs):
    n_x = sum(X_PARTS)
    x_refs, spare_refs, g_refs = refs[:n_x], refs[n_x : 2 * n_x], refs[2 * n_x : 2 * n_x + N_DP]
    gate_ref, up_ref, turned_ref = refs[2 * n_x + N_DP :]
    step = pl.program_id(0)

    @pl.when(step == 0)
    def _():
        for g in range(N_DP):
            turned = g_refs[g][...].astype(F32).T.astype(BF)
            turned_ref[:, g * ROWS : (g + 1) * ROWS] = turned[:, :ROWS]
            turned_ref[:, N_DP * ROWS + g * EXP : N_DP * ROWS + (g + 1) * EXP] = turned[:, ROWS:]

    spares = []
    total = jnp.zeros((2 * HS, SEG), F32)
    at = 0
    for x_ref, spare_ref in zip(x_refs, spare_refs):
        n = x_ref.shape[0]
        pick = one(iota((n // MAIN, n), 1) == iota((n // MAIN, n), 0) * MAIN + step).astype(BF)
        spares.append(dot(pick, spare_ref[...]).astype(BF))
        total = total + dot(turned_ref[:, at : at + n], x_ref[...])
        at += n
    total = total + dot(turned_ref[:, at:], jnp.concatenate(spares, axis=0))
    gate_ref[...] = total[:HS].astype(BF)
    up_ref[...] = total[HS:].astype(BF)


def gate_up_terms(xs, gs):
    mains = [pl.BlockSpec((x.shape[0], SEG), lambda j: (0, j)) for x in xs]
    spares = [pl.BlockSpec((x.shape[0], SEG), lambda j: (0, MAIN)) for x in xs]
    grad = pl.BlockSpec((ALL, 2 * HS), lambda j: (0, 0))
    out = pl.BlockSpec((HS, SEG), lambda j: (0, j))
    shape = jax.ShapeDtypeStruct((HS, D), BF)
    return pl.pallas_call(
        gate_up_kernel,
        grid=(MAIN,),
        in_specs=mains + spares + [grad] * N_DP,
        out_specs=[out, out],
        out_shape=[shape, shape],
        scratch_shapes=[pltpu.VMEM((2 * HS, N_DP * ALL), BF)],
        name="gate_up_terms",
    )(*xs, *xs, *gs)


def combine_kernel(ids_ref, probs_ref, recv_ref, rows_ref, probs_grad_ref, recv_v, sem):
    halves = [
        start(recv_ref.at[pl.ds(h * HALF, HALF)], recv_v.at[pl.ds(h * HALF, HALF)], sem.at[h])
        for h in range(2)
    ]
    ids = jnp.concatenate(
        [ids_ref[...].astype(F32), jnp.zeros((8 - TOP, TOK), F32)], axis=0
    ).T.astype(jnp.int32)
    lane_e = iota((TOK, EXP), 1)
    member = ids[:, 0:1] == lane_e
    for k in range(1, TOP):
        member = member | (ids[:, k : k + 1] == lane_e)
    before = one(iota((TOK, TOK), 1) < iota((TOK, TOK), 0)).astype(BF)
    rank = jnp.where(member, dot(before, one(member).astype(BF)), 200.0)
    slot = iota((TOK, ROWS), 1)
    spread = one(iota((EXP, ROWS), 0) == (iota((EXP, ROWS), 1) >> 3)).astype(BF)
    rank_slots = dot(rank.astype(BF), spread)
    sub = slot & (MAIN - 1)
    main = rank_slots == sub.astype(F32)
    ninth = rank_slots == float(MAIN)
    main_bf = one(main).astype(BF)
    spare = jnp.concatenate([one(ninth & (sub == j)).astype(BF) for j in range(MAIN)], axis=0)
    for copy in halves:
        copy.wait()
    extra = dot(spare, recv_v[:, D : D + SEG])
    for j in range(MAIN):
        at = slice(j * SEG, (j + 1) * SEG)
        part = dot(main_bf, recv_v[:, at])
        rows_ref[:, at] = (part + extra[j * TOK : (j + 1) * TOK, :]).astype(BF)
    lanes = one(iota((8, 128), 0) == iota((8, 128), 1)).astype(BF)
    values = dot_nt(lanes, recv_v[:, D + SEG :])
    per_slot = jnp.where(main, values[0:1] + values[1:2], 0.0)
    per_slot = per_slot + jnp.where(ninth & (sub == 0), values[2:3] + values[3:4], 0.0)
    lane_k = iota((TOK, 8), 1)
    found = jnp.zeros((TOK, 8), F32)
    for k in range(TOP):
        hit = ids[:, k : k + 1] == (slot >> 3)
        value = jnp.sum(jnp.where(hit, per_slot, 0.0), axis=1, keepdims=True)
        found = jnp.where(lane_k == k, value, found)
    probs_grad_ref[...] = found.T[:TOP] / probs_ref[...].astype(F32)


def combine(ids, probs, recv):
    vmem = pl.BlockSpec(memory_space=pltpu.VMEM)
    return pl.pallas_call(
        combine_kernel,
        in_specs=[vmem, vmem, pl.BlockSpec(memory_space=pltpu.HBM)],
        out_specs=[vmem, vmem],
        out_shape=[
            jax.ShapeDtypeStruct((TOK, D), BF),
            jax.ShapeDtypeStruct((TOP, TOK), F32),
        ],
        scratch_shapes=[pltpu.VMEM((ROWS, Y_COLS), BF), pltpu.SemaphoreType.DMA((2,))],
        name="combine",
    )(ids, probs, recv)


def exchange(flat):
    out = lax.all_to_all(
        flat.reshape(EXP, MAIN, flat.shape[1]), "expert", split_axis=0, concat_axis=0, tiled=True
    )
    return out.reshape(flat.shape)


def shift(value, by):
    return lax.ppermute(value, "dp", [(i, (i + by) % N_DP) for i in range(N_DP)])


def gather_rows(recv):
    top, low = recv[:HALF], recv[HALF:]
    prev_top = shift(top, 1)
    next_low = shift(low, 3)
    prev_low = shift(low, 1)
    next_top = shift(top, 3)
    far_top = shift(prev_top, 1)
    far_low = shift(next_low, 3)
    return [recv, prev_top, prev_low, far_top, far_low, next_top, next_low]


def per_device(tokens, out_grad, gate_probs, expert_ids, w_gate, w_up, w_down):
    own = lax.axis_index("dp").astype(jnp.int32).reshape(1)
    ids = expert_ids.T
    gate_mat, up_mat, down_mat = w_gate[0], w_up[0], w_down[0]
    recv_x = exchange(pack(pack_x_kernel, ids, tokens))
    probs = gate_probs.T
    recv_dy = exchange(pack(pack_dy_kernel, ids, out_grad, probs))
    xs = gather_rows(recv_x)
    slope, silu, act, turned = forward(recv_x, gate_mat, up_mat)
    back, *pieces = rows_pass(own, recv_dy, down_mat, slope, silu, act, gate_mat, up_mat)
    back_rows = exchange(back)
    gs = [pieces[0]] + [shift(pieces[d], d) for d in range(1, N_DP)]
    terms = down_terms(own, turned, recv_dy)
    downs = [terms[0]] + [shift(terms[d], d) for d in range(1, N_DP)]
    gate_grad, up_grad = gate_up_terms(xs, gs)
    down_grad = downs[0].astype(F32)
    for d in range(1, N_DP):
        down_grad = down_grad + downs[d].astype(F32)
    tokens_grad, probs_grad = combine(ids, probs, back_rows)
    return (
        tokens_grad,
        probs_grad.T,
        gate_grad.T[None],
        up_grad.T[None],
        down_grad.astype(BF)[None],
    )


def solution(mesh):
    rows = P(("dp", "expert"), None)
    weights = P("expert", None, None)
    return jax.shard_map(
        per_device,
        mesh=mesh,
        in_specs=(rows, rows, rows, rows, weights, weights, weights),
        out_specs=(rows, rows, P("expert", None, "dp"), P("expert", None, "dp"), P("expert", "dp", None)),
        check_vma=False,
    )
```

```python
import jax
import jax.numpy as jnp
from jax import lax
from jax.experimental import pallas as pl
from jax.experimental.pallas import tpu as pltpu
from jax.sharding import PartitionSpec as P


BF = jnp.bfloat16
F32 = jnp.float32
TOP = 4
TOK = 128
EXP = 64
MAIN = 8
ROWS = EXP * MAIN
ALL = ROWS + EXP
D = 2048
H = 768
SEG = D // MAIN
N_DP = 4
HS = H // N_DP
X_COLS = D + SEG
Y_COLS = D + SEG + 128


def dot(a, b):
    return jnp.dot(a, b, preferred_element_type=F32)


def dot_nt(a, b):
    return lax.dot_general(a, b, (((1,), (1,)), ((), ())), preferred_element_type=F32)


def iota(shape, axis):
    return lax.broadcasted_iota(jnp.int32, shape, axis)


def one(mask):
    return jnp.where(mask, 1.0, 0.0)


PACK_STEPS = 2
PACK = ROWS // PACK_STEPS


def pack_rows(ids_ref, data_ref, out_ref, rank_ref, probs_ref=None, chosen_ref=None):
    step = pl.program_id(0)

    @pl.when(step == 0)
    def _():
        ids = ids_ref[...]
        lane_e = iota((EXP, TOK), 0)
        picks = [ids[k : k + 1, :] == lane_e for k in range(TOP)]
        member = picks[0] | picks[1] | picks[2] | picks[3]
        before = one(iota((TOK, TOK), 0) < iota((TOK, TOK), 1)).astype(BF)
        rank_ref[...] = jnp.where(member, dot(one(member).astype(BF), before), 200.0).astype(BF)
        if probs_ref is not None:
            probs = probs_ref[...].astype(F32)
            chosen = jnp.zeros((EXP, TOK), F32)
            for k in range(TOP):
                chosen = chosen + jnp.where(picks[k], probs[k : k + 1, :], 0.0)
            chosen_ref[...] = chosen.astype(BF)

    expert = (iota((PACK, EXP), 0) >> 3) + step * (PACK // MAIN)
    spread = one(expert == iota((PACK, EXP), 1)).astype(BF)
    rank_rows = dot(spread, rank_ref[...])
    sub = iota((PACK, TOK), 0) & (MAIN - 1)
    main = rank_rows == sub.astype(F32)
    ninth = rank_rows == float(MAIN)
    spare = jnp.concatenate([one(ninth & (sub == j)).astype(BF) for j in range(MAIN)], axis=1)
    parts = jnp.concatenate([data_ref[:, j * SEG : (j + 1) * SEG] for j in range(MAIN)], axis=0)
    rows = dot(one(main).astype(BF), data_ref[...])
    extra = dot(spare, parts)
    if probs_ref is not None:
        prob_rows = dot(spread, chosen_ref[...])
        rows = rows * jnp.sum(jnp.where(main, prob_rows, 0.0), axis=1, keepdims=True)
        extra = extra * jnp.sum(jnp.where(ninth, prob_rows, 0.0), axis=1, keepdims=True)
    out_ref[:, :D] = rows.astype(BF)
    out_ref[:, D:] = extra.astype(BF)


def pack_x_kernel(ids_ref, data_ref, out_ref, rank_ref):
    pack_rows(ids_ref, data_ref, out_ref, rank_ref)


def pack_dy_kernel(ids_ref, data_ref, probs_ref, out_ref, rank_ref, chosen_ref):
    pack_rows(ids_ref, data_ref, out_ref, rank_ref, probs_ref, chosen_ref)


def pack(kernel, *args):
    return pl.pallas_call(
        kernel,
        grid=(PACK_STEPS,),
        in_specs=[pl.BlockSpec(x.shape, lambda j: (0, 0)) for x in args],
        out_specs=pl.BlockSpec((PACK, X_COLS), lambda j: (j, 0)),
        out_shape=jax.ShapeDtypeStruct((ROWS, X_COLS), BF),
        scratch_shapes=[pltpu.VMEM((EXP, TOK), BF)] * (len(args) - 1),
    )(*args)


def unfold_mask():
    row = iota((ROWS, ROWS), 0)
    col = iota((ROWS, ROWS), 1)
    return one(col == (row & (EXP - 1)) * MAIN + (row >> 6)).astype(BF)


def fold_mask():
    row = iota((ROWS, ROWS), 0)
    col = iota((ROWS, ROWS), 1)
    return one(col == (row & (MAIN - 1)) * EXP + (row >> 3)).astype(BF)


def fill_rows(recv_ref, rows_ref):
    rows_ref[:ROWS, :] = recv_ref[:, :D]
    spare = dot(unfold_mask(), recv_ref[:, D : D + SEG]).astype(BF)
    for j in range(MAIN):
        rows_ref[ROWS:, j * SEG : (j + 1) * SEG] = spare[j * EXP : (j + 1) * EXP, :]


def forward_kernel(
    recv_ref, gate_ref, up_ref, slope_ref, silu_ref, act_ref, turned_ref, rows_ref
):
    @pl.when(pl.program_id(0) == 0)
    def _():
        fill_rows(recv_ref, rows_ref)

    gate_pre = dot(rows_ref[...], gate_ref[...])
    up_pre = dot(rows_ref[...], up_ref[...])
    sig = jax.nn.sigmoid(gate_pre)
    silu = gate_pre * sig
    silu_ref[...] = silu
    act = silu * up_pre
    act_ref[...] = act
    turned_ref[...] = act.T.astype(BF)
    slope_ref[...] = up_pre * sig * (1.0 + gate_pre * (1.0 - sig))


def forward(recv_x, gate_mat, up_mat):
    full = pl.BlockSpec((ROWS, X_COLS), lambda j: (0, 0))
    weight = pl.BlockSpec((D, 256), lambda j: (0, j))
    out = pl.BlockSpec((ALL, 256), lambda j: (0, j))
    shape = jax.ShapeDtypeStruct((ALL, H), F32)
    return pl.pallas_call(
        forward_kernel,
        grid=(H // 256,),
        in_specs=[full, weight, weight],
        out_specs=[out, out, out, pl.BlockSpec((256, ALL), lambda j: (j, 0))],
        out_shape=[shape, shape, shape, jax.ShapeDtypeStruct((H, ALL), BF)],
        scratch_shapes=[pltpu.VMEM((ALL, D), BF)],
        name="forward",
    )(recv_x, gate_mat, up_mat)


def fill_spare(rows_ref, spare_ref):
    spare = dot(unfold_mask(), spare_ref[...]).astype(BF)
    for j in range(MAIN):
        rows_ref[ROWS:, j * SEG : (j + 1) * SEG] = spare[j * EXP : (j + 1) * EXP, :]


def start(source, target, sem):
    copy = pltpu.make_async_copy(source, target, sem)
    copy.start()
    return copy


def cols(ref, first, count):
    return ref.at[:, pl.ds(first, count)]


def rows_kernel(
    own_ref, recv_ref, down_ref, slope_ref, silu_ref, act_ref, gate_ref, up_ref,
    back_ref, piece0_ref, piece1_ref, piece2_ref, piece3_ref,
    rows_v, extra_v, down_v, slope_v, silu_v, act_v, weight_v, grad_v, piece_v, back_v, spare_v,
    sem_in, sem_out,
):
    pieces = [piece0_ref, piece1_ref, piece2_ref, piece3_ref]
    first = [
        start(cols(recv_ref, 0, D), rows_v.at[pl.ds(0, ROWS)], sem_in.at[0]),
        start(cols(recv_ref, D, SEG), extra_v, sem_in.at[1]),
    ]
    down_in = start(down_ref, down_v, sem_in.at[2])
    terms_in = [
        start(act_ref, act_v, sem_in.at[3]),
        start(slope_ref, slope_v, sem_in.at[4]),
        start(silu_ref, silu_v, sem_in.at[5]),
    ]
    for copy in first:
        copy.wait()
    weights_in = [
        start(gate_ref, cols(weight_v, 0, H), sem_in.at[6]),
        start(up_ref, cols(weight_v, H, H), sem_in.at[7]),
    ]
    fill_spare(rows_v, extra_v)
    down_in.wait()
    grad_hidden = dot_nt(rows_v[...], down_v[...])
    for copy in terms_in:
        copy.wait()
    total = jnp.sum(act_v[...] * grad_hidden, axis=1, keepdims=True)
    grad_v[:, :H] = (grad_hidden * slope_v[...]).astype(BF)
    grad_v[:, H:] = (grad_hidden * silu_v[...]).astype(BF)
    for copy in weights_in:
        copy.wait()
    outs = []
    own = own_ref[0]
    for q in range(4):
        n = D // 4
        row = dot_nt(grad_v[...], weight_v[q * n : (q + 1) * n, :]).astype(BF)
        back_v[:, q * n : (q + 1) * n] = row[:ROWS]
        for j in range(MAIN // 4):
            at = (q * (MAIN // 4) + j) * EXP
            spare_v[at : at + EXP, :] = row[ROWS:, j * SEG : (j + 1) * SEG]
        outs.append(start(cols(back_v, q * n, n), cols(back_ref, q * n, n), sem_out.at[q]))
        if q == 0:
            for t in range(N_DP):
                piece_v[t, :, :HS] = grad_v[:, t * HS : (t + 1) * HS]
                piece_v[t, :, HS:] = grad_v[:, H + t * HS : H + (t + 1) * HS]
            for d in range(N_DP):
                t = lax.rem(own + d, N_DP)
                outs.append(start(piece_v.at[t], pieces[d], sem_out.at[4 + d]))
    back_v[:, D : D + SEG] = dot(fold_mask(), spare_v[...]).astype(BF)
    high = total.astype(BF)
    low = (total - high.astype(F32)).astype(BF)
    lane = iota((EXP, 128), 1)
    ninth = jnp.where(
        lane == 2,
        high[ROWS:].astype(F32),
        jnp.where(lane == 3, low[ROWS:].astype(F32), 0.0),
    ).astype(BF)
    spread = one((iota((ROWS, EXP), 0) >> 3) == iota((ROWS, EXP), 1)).astype(BF)
    lane_rows = iota((ROWS, 128), 1)
    back_v[:, D + SEG :] = jnp.where(
        lane_rows == 0,
        high[:ROWS].astype(F32),
        jnp.where(lane_rows == 1, low[:ROWS].astype(F32), dot(spread, ninth)),
    ).astype(BF)
    outs.append(start(cols(back_v, D, SEG + 128), cols(back_ref, D, SEG + 128), sem_out.at[8]))
    for copy in outs:
        copy.wait()


def rows_pass(own, recv_dy, down_mat, slope, silu, act, gate_mat, up_mat):
    hbm = pl.BlockSpec(memory_space=pltpu.HBM)
    piece = jax.ShapeDtypeStruct((ALL, 2 * HS), BF)
    return pl.pallas_call(
        rows_kernel,
        in_specs=[pl.BlockSpec(memory_space=pltpu.SMEM)] + [hbm] * 7,
        out_specs=[hbm] * (1 + N_DP),
        out_shape=[jax.ShapeDtypeStruct((ROWS, Y_COLS), BF)] + [piece] * N_DP,
        scratch_shapes=[
            pltpu.VMEM((ALL, D), BF),
            pltpu.VMEM((ROWS, SEG), BF),
            pltpu.VMEM((H, D), BF),
            pltpu.VMEM((ALL, H), F32),
            pltpu.VMEM((ALL, H), F32),
            pltpu.VMEM((ALL, H), F32),
            pltpu.VMEM((D, 2 * H), BF),
            pltpu.VMEM((ALL, 2 * H), BF),
            pltpu.VMEM((N_DP, ALL, 2 * HS), BF),
            pltpu.VMEM((ROWS, Y_COLS), BF),
            pltpu.VMEM((ROWS, SEG), BF),
            pltpu.SemaphoreType.DMA((8,)),
            pltpu.SemaphoreType.DMA((9,)),
        ],
        name="rows_pass",
    )(own, recv_dy, down_mat, slope, silu, act, gate_mat, up_mat)


HALF_H = HS // 2


def down_kernel(
    own_ref, turned_ref, recv_ref, same_ref, next_ref, far_top_ref, far_low_ref, prev_ref,
    rows_v, extra_v, turned_v, out_v, sem_in, sem_out,
):
    ins = [
        start(cols(recv_ref, D, SEG), extra_v, sem_in.at[1]),
        start(cols(recv_ref, 0, D), rows_v.at[pl.ds(0, ROWS)], sem_in.at[0]),
        start(turned_ref, turned_v, sem_in.at[2]),
    ]
    ins[0].wait()
    fill_spare(rows_v, extra_v)
    ins[1].wait()
    ins[2].wait()
    outs = []
    for d in (2, 1, 3, 0):
        at = pl.multiple_of(lax.rem(own_ref[0] + d, N_DP) * HS, HS)
        out_v[d] = dot(turned_v[pl.ds(at, HS), :], rows_v[...]).astype(BF)
        if d == 2:
            top, low = out_v.at[d, pl.ds(0, HALF_H)], out_v.at[d, pl.ds(HALF_H, HALF_H)]
            outs.append(start(top, far_top_ref, sem_out.at[d]))
            outs.append(start(low, far_low_ref, sem_out.at[N_DP]))
        else:
            target = {0: same_ref, 1: next_ref, 3: prev_ref}[d]
            outs.append(start(out_v.at[d], target, sem_out.at[d]))
    for copy in outs:
        copy.wait()


def down_terms(own, turned, recv_dy):
    hbm = pl.BlockSpec(memory_space=pltpu.HBM)
    rows = [HS, HS, HALF_H, HALF_H, HS]
    return pl.pallas_call(
        down_kernel,
        in_specs=[pl.BlockSpec(memory_space=pltpu.SMEM), hbm, hbm],
        out_specs=[hbm] * len(rows),
        out_shape=[jax.ShapeDtypeStruct((n, D), BF) for n in rows],
        scratch_shapes=[
            pltpu.VMEM((ALL, D), BF),
            pltpu.VMEM((ROWS, SEG), BF),
            pltpu.VMEM((H, ALL), BF),
            pltpu.VMEM((N_DP, HS, D), BF),
            pltpu.SemaphoreType.DMA((3,)),
            pltpu.SemaphoreType.DMA((N_DP + 1,)),
        ],
        name="down_terms",
    )(own, turned, recv_dy)


def merge_kernel(next_ref, prev_ref, from_prev_ref, from_next_ref, next_out_ref, prev_out_ref):
    top = next_ref[:HALF_H].astype(F32) + from_prev_ref[...].astype(F32)
    next_out_ref[:HALF_H] = top.astype(BF)
    next_out_ref[HALF_H:] = next_ref[HALF_H:]
    low = prev_ref[HALF_H:].astype(F32) + from_next_ref[...].astype(F32)
    prev_out_ref[:HALF_H] = prev_ref[:HALF_H]
    prev_out_ref[HALF_H:] = low.astype(BF)


def merge(*args):
    shape = jax.ShapeDtypeStruct((HS, D), BF)
    return pl.pallas_call(merge_kernel, out_shape=[shape, shape], name="merge")(*args)


HALF = ROWS // 2
X_PARTS = (1, 2, 2, 2)


def gate_up_kernel(*refs):
    n_x = sum(X_PARTS)
    x_refs, spare_refs, g_refs = refs[:n_x], refs[n_x : 2 * n_x], refs[2 * n_x : 2 * n_x + N_DP]
    gate_ref, up_ref, turned_ref = refs[2 * n_x + N_DP :]
    step = pl.program_id(0)

    @pl.when(step == 0)
    def _():
        for g in range(N_DP):
            turned = g_refs[g][...].astype(F32).T.astype(BF)
            turned_ref[:, g * ROWS : (g + 1) * ROWS] = turned[:, :ROWS]
            turned_ref[:, N_DP * ROWS + g * EXP : N_DP * ROWS + (g + 1) * EXP] = turned[:, ROWS:]

    spares = []
    total = jnp.zeros((2 * HS, SEG), F32)
    at = 0
    for x_ref, spare_ref in zip(x_refs, spare_refs):
        n = x_ref.shape[0]
        pick = one(iota((n // MAIN, n), 1) == iota((n // MAIN, n), 0) * MAIN + step).astype(BF)
        spares.append(dot(pick, spare_ref[...]).astype(BF))
        total = total + dot(turned_ref[:, at : at + n], x_ref[...])
        at += n
    total = total + dot(turned_ref[:, at:], jnp.concatenate(spares, axis=0))
    gate_ref[...] = total[:HS].astype(BF)
    up_ref[...] = total[HS:].astype(BF)


def gate_up_terms(xs, gs):
    mains = [pl.BlockSpec((x.shape[0], SEG), lambda j: (0, j)) for x in xs]
    spares = [pl.BlockSpec((x.shape[0], SEG), lambda j: (0, MAIN)) for x in xs]
    grad = pl.BlockSpec((ALL, 2 * HS), lambda j: (0, 0))
    out = pl.BlockSpec((HS, SEG), lambda j: (0, j))
    shape = jax.ShapeDtypeStruct((HS, D), BF)
    return pl.pallas_call(
        gate_up_kernel,
        grid=(MAIN,),
        in_specs=mains + spares + [grad] * N_DP,
        out_specs=[out, out],
        out_shape=[shape, shape],
        scratch_shapes=[pltpu.VMEM((2 * HS, N_DP * ALL), BF)],
        compiler_params=pltpu.CompilerParams(vmem_limit_bytes=65 * 1024 * 1000),
        name="gate_up_terms",
    )(*xs, *xs, *gs)


def combine_kernel(ids_ref, probs_ref, recv_ref, rows_ref, probs_grad_ref, recv_v, sem):
    halves = [
        start(recv_ref.at[pl.ds(h * HALF, HALF)], recv_v.at[pl.ds(h * HALF, HALF)], sem.at[h])
        for h in range(2)
    ]
    ids = jnp.concatenate(
        [ids_ref[...].astype(F32), jnp.zeros((8 - TOP, TOK), F32)], axis=0
    ).T.astype(jnp.int32)
    lane_e = iota((TOK, EXP), 1)
    member = ids[:, 0:1] == lane_e
    for k in range(1, TOP):
        member = member | (ids[:, k : k + 1] == lane_e)
    before = one(iota((TOK, TOK), 1) < iota((TOK, TOK), 0)).astype(BF)
    rank = jnp.where(member, dot(before, one(member).astype(BF)), 200.0)
    slot = iota((TOK, ROWS), 1)
    spread = one(iota((EXP, ROWS), 0) == (iota((EXP, ROWS), 1) >> 3)).astype(BF)
    rank_slots = dot(rank.astype(BF), spread)
    sub = slot & (MAIN - 1)
    main = rank_slots == sub.astype(F32)
    ninth = rank_slots == float(MAIN)
    main_bf = one(main).astype(BF)
    spare = jnp.concatenate([one(ninth & (sub == j)).astype(BF) for j in range(MAIN)], axis=0)
    for copy in halves:
        copy.wait()
    extra = dot(spare, recv_v[:, D : D + SEG])
    for j in range(MAIN):
        at = slice(j * SEG, (j + 1) * SEG)
        part = dot(main_bf, recv_v[:, at])
        rows_ref[:, at] = (part + extra[j * TOK : (j + 1) * TOK, :]).astype(BF)
    lanes = one(iota((8, 128), 0) == iota((8, 128), 1)).astype(BF)
    values = dot_nt(lanes, recv_v[:, D + SEG :])
    per_slot = jnp.where(main, values[0:1] + values[1:2], 0.0)
    per_slot = per_slot + jnp.where(ninth & (sub == 0), values[2:3] + values[3:4], 0.0)
    lane_k = iota((TOK, 8), 1)
    found = jnp.zeros((TOK, 8), F32)
    for k in range(TOP):
        hit = ids[:, k : k + 1] == (slot >> 3)
        value = jnp.sum(jnp.where(hit, per_slot, 0.0), axis=1, keepdims=True)
        found = jnp.where(lane_k == k, value, found)
    probs_grad_ref[...] = found.T[:TOP] / probs_ref[...].astype(F32)


def combine(ids, probs, recv):
    vmem = pl.BlockSpec(memory_space=pltpu.VMEM)
    return pl.pallas_call(
        combine_kernel,
        in_specs=[vmem, vmem, pl.BlockSpec(memory_space=pltpu.HBM)],
        out_specs=[vmem, vmem],
        out_shape=[
            jax.ShapeDtypeStruct((TOK, D), BF),
            jax.ShapeDtypeStruct((TOP, TOK), F32),
        ],
        scratch_shapes=[pltpu.VMEM((ROWS, Y_COLS), BF), pltpu.SemaphoreType.DMA((2,))],
        name="combine",
    )(ids, probs, recv)


def exchange(flat):
    out = lax.all_to_all(
        flat.reshape(EXP, MAIN, flat.shape[1]), "expert", split_axis=0, concat_axis=0, tiled=True
    )
    return out.reshape(flat.shape)


def shift(value, by):
    return lax.ppermute(value, "dp", [(i, (i + by) % N_DP) for i in range(N_DP)])


def gather_rows(recv):
    top, low = recv[:HALF], recv[HALF:]
    prev_top = shift(top, 1)
    next_low = shift(low, 3)
    prev_low = shift(low, 1)
    next_top = shift(top, 3)
    far_top = shift(prev_top, 1)
    far_low = shift(next_low, 3)
    return [recv, prev_top, prev_low, far_top, far_low, next_top, next_low]


def per_device(tokens, out_grad, gate_probs, expert_ids, w_gate, w_up, w_down):
    own = lax.axis_index("dp").astype(jnp.int32).reshape(1)
    ids = expert_ids.T
    gate_mat, up_mat, down_mat = w_gate[0], w_up[0], w_down[0]
    recv_x = exchange(pack(pack_x_kernel, ids, tokens))
    probs = gate_probs.T
    recv_dy = exchange(pack(pack_dy_kernel, ids, out_grad, probs))
    xs = gather_rows(recv_x)
    slope, silu, act, turned = forward(recv_x, gate_mat, up_mat)
    back, *pieces = rows_pass(own, recv_dy, down_mat, slope, silu, act, gate_mat, up_mat)
    back_rows = exchange(back)
    gs = [pieces[0]] + [shift(pieces[d], d) for d in range(1, N_DP)]
    terms = down_terms(own, turned, recv_dy)
    own_term, next_term, far_top, far_low, prev_term = terms
    from_prev = shift(far_top, 1)
    from_next = shift(far_low, 3)
    next_term, prev_term = merge(next_term, prev_term, from_prev, from_next)
    downs = [own_term, shift(next_term, 1), shift(prev_term, 3)]
    gate_grad, up_grad = gate_up_terms(xs, gs)
    down_grad = downs[0].astype(F32)
    for term in downs[1:]:
        down_grad = down_grad + term.astype(F32)
    tokens_grad, probs_grad = combine(ids, probs, back_rows)
    return (
        tokens_grad,
        probs_grad.T,
        gate_grad.T[None],
        up_grad.T[None],
        down_grad.astype(BF)[None],
    )


def solution(mesh):
    rows = P(("dp", "expert"), None)
    weights = P("expert", None, None)
    return jax.shard_map(
        per_device,
        mesh=mesh,
        in_specs=(rows, rows, rows, rows, weights, weights, weights),
        out_specs=(rows, rows, P("expert", None, "dp"), P("expert", None, "dp"), P("expert", "dp", None)),
        check_vma=False,
    )
```

```python
import jax
import jax.numpy as jnp
from jax import lax
from jax.experimental import pallas as pl
from jax.experimental.pallas import tpu as pltpu
from jax.sharding import PartitionSpec as P


BF = jnp.bfloat16
F32 = jnp.float32
TOP = 4
TOK = 128
EXP = 64
MAIN = 8
ROWS = EXP * MAIN
ALL = ROWS + EXP
D = 2048
H = 768
SEG = D // MAIN
N_DP = 4
HS = H // N_DP
X_COLS = D + SEG
Y_COLS = D + SEG + 128


def dot(a, b):
    return jnp.dot(a, b, preferred_element_type=F32)


def dot_nt(a, b):
    return lax.dot_general(a, b, (((1,), (1,)), ((), ())), preferred_element_type=F32)


def iota(shape, axis):
    return lax.broadcasted_iota(jnp.int32, shape, axis)


def one(mask):
    return jnp.where(mask, 1.0, 0.0)


PACK_STEPS = 2
PACK = ROWS // PACK_STEPS


def pack_rows(ids_ref, data_ref, out_ref, rank_ref, probs_ref=None, chosen_ref=None):
    step = pl.program_id(0)

    @pl.when(step == 0)
    def _():
        ids = ids_ref[...]
        lane_e = iota((EXP, TOK), 0)
        picks = [ids[k : k + 1, :] == lane_e for k in range(TOP)]
        member = picks[0] | picks[1] | picks[2] | picks[3]
        before = one(iota((TOK, TOK), 0) < iota((TOK, TOK), 1)).astype(BF)
        rank_ref[...] = jnp.where(member, dot(one(member).astype(BF), before), 200.0).astype(BF)
        if probs_ref is not None:
            probs = probs_ref[...].astype(F32)
            chosen = jnp.zeros((EXP, TOK), F32)
            for k in range(TOP):
                chosen = chosen + jnp.where(picks[k], probs[k : k + 1, :], 0.0)
            chosen_ref[...] = chosen.astype(BF)

    expert = (iota((PACK, EXP), 0) >> 3) + step * (PACK // MAIN)
    spread = one(expert == iota((PACK, EXP), 1)).astype(BF)
    rank_rows = dot(spread, rank_ref[...])
    sub = iota((PACK, TOK), 0) & (MAIN - 1)
    main = rank_rows == sub.astype(F32)
    ninth = rank_rows == float(MAIN)
    spare = jnp.concatenate([one(ninth & (sub == j)).astype(BF) for j in range(MAIN)], axis=1)
    parts = jnp.concatenate([data_ref[:, j * SEG : (j + 1) * SEG] for j in range(MAIN)], axis=0)
    rows = dot(one(main).astype(BF), data_ref[...])
    extra = dot(spare, parts)
    if probs_ref is not None:
        prob_rows = dot(spread, chosen_ref[...])
        rows = rows * jnp.sum(jnp.where(main, prob_rows, 0.0), axis=1, keepdims=True)
        extra = extra * jnp.sum(jnp.where(ninth, prob_rows, 0.0), axis=1, keepdims=True)
    out_ref[:, :D] = rows.astype(BF)
    out_ref[:, D:] = extra.astype(BF)


def pack_x_kernel(ids_ref, data_ref, out_ref, rank_ref):
    pack_rows(ids_ref, data_ref, out_ref, rank_ref)


def pack_dy_kernel(ids_ref, data_ref, probs_ref, out_ref, rank_ref, chosen_ref):
    pack_rows(ids_ref, data_ref, out_ref, rank_ref, probs_ref, chosen_ref)


def pack(kernel, *args):
    return pl.pallas_call(
        kernel,
        grid=(PACK_STEPS,),
        in_specs=[pl.BlockSpec(x.shape, lambda j: (0, 0)) for x in args],
        out_specs=pl.BlockSpec((PACK, X_COLS), lambda j: (j, 0)),
        out_shape=jax.ShapeDtypeStruct((ROWS, X_COLS), BF),
        scratch_shapes=[pltpu.VMEM((EXP, TOK), BF)] * (len(args) - 1),
    )(*args)


def unfold_mask():
    row = iota((ROWS, ROWS), 0)
    col = iota((ROWS, ROWS), 1)
    return one(col == (row & (EXP - 1)) * MAIN + (row >> 6)).astype(BF)


def fold_mask():
    row = iota((ROWS, ROWS), 0)
    col = iota((ROWS, ROWS), 1)
    return one(col == (row & (MAIN - 1)) * EXP + (row >> 3)).astype(BF)


def fill_rows(recv_ref, rows_ref):
    rows_ref[:ROWS, :] = recv_ref[:, :D]
    spare = dot(unfold_mask(), recv_ref[:, D : D + SEG]).astype(BF)
    for j in range(MAIN):
        rows_ref[ROWS:, j * SEG : (j + 1) * SEG] = spare[j * EXP : (j + 1) * EXP, :]


def forward_kernel(
    recv_ref, gate_ref, up_ref, slope_ref, silu_ref, act_ref, turned_ref, rows_ref
):
    @pl.when(pl.program_id(0) == 0)
    def _():
        fill_rows(recv_ref, rows_ref)

    gate_pre = dot(rows_ref[...], gate_ref[...])
    up_pre = dot(rows_ref[...], up_ref[...])
    sig = jax.nn.sigmoid(gate_pre)
    silu = gate_pre * sig
    silu_ref[...] = silu
    act = silu * up_pre
    act_ref[...] = act
    turned_ref[...] = act.T.astype(BF)
    slope_ref[...] = up_pre * sig * (1.0 + gate_pre * (1.0 - sig))


def forward(recv_x, gate_mat, up_mat):
    full = pl.BlockSpec((ROWS, X_COLS), lambda j: (0, 0))
    weight = pl.BlockSpec((D, 256), lambda j: (0, j))
    out = pl.BlockSpec((ALL, 256), lambda j: (0, j))
    shape = jax.ShapeDtypeStruct((ALL, H), F32)
    return pl.pallas_call(
        forward_kernel,
        grid=(H // 256,),
        in_specs=[full, weight, weight],
        out_specs=[out, out, out, pl.BlockSpec((256, ALL), lambda j: (j, 0))],
        out_shape=[shape, shape, shape, jax.ShapeDtypeStruct((H, ALL), BF)],
        scratch_shapes=[pltpu.VMEM((ALL, D), BF)],
        name="forward",
    )(recv_x, gate_mat, up_mat)


def fill_spare(rows_ref, spare_ref):
    spare = dot(unfold_mask(), spare_ref[...]).astype(BF)
    for j in range(MAIN):
        rows_ref[ROWS:, j * SEG : (j + 1) * SEG] = spare[j * EXP : (j + 1) * EXP, :]


def start(source, target, sem):
    copy = pltpu.make_async_copy(source, target, sem)
    copy.start()
    return copy


def cols(ref, first, count):
    return ref.at[:, pl.ds(first, count)]


def rows_kernel(
    own_ref, recv_ref, down_ref, slope_ref, silu_ref, act_ref, gate_ref, up_ref,
    back_ref, piece0_ref, piece1_ref, piece2_ref, piece3_ref,
    rows_v, extra_v, down_v, slope_v, silu_v, act_v, weight_v, grad_v, piece_v, back_v, spare_v,
    sem_in, sem_out,
):
    pieces = [piece0_ref, piece1_ref, piece2_ref, piece3_ref]
    first = [
        start(cols(recv_ref, 0, D), rows_v.at[pl.ds(0, ROWS)], sem_in.at[0]),
        start(cols(recv_ref, D, SEG), extra_v, sem_in.at[1]),
    ]
    down_in = start(down_ref, down_v, sem_in.at[2])
    terms_in = [
        start(act_ref, act_v, sem_in.at[3]),
        start(slope_ref, slope_v, sem_in.at[4]),
        start(silu_ref, silu_v, sem_in.at[5]),
    ]
    for copy in first:
        copy.wait()
    weights_in = [
        start(gate_ref, cols(weight_v, 0, H), sem_in.at[6]),
        start(up_ref, cols(weight_v, H, H), sem_in.at[7]),
    ]
    fill_spare(rows_v, extra_v)
    down_in.wait()
    grad_hidden = dot_nt(rows_v[...], down_v[...])
    for copy in terms_in:
        copy.wait()
    total = jnp.sum(act_v[...] * grad_hidden, axis=1, keepdims=True)
    grad_v[:, :H] = (grad_hidden * slope_v[...]).astype(BF)
    grad_v[:, H:] = (grad_hidden * silu_v[...]).astype(BF)
    for copy in weights_in:
        copy.wait()
    outs = []
    own = own_ref[0]
    for q in range(4):
        n = D // 4
        row = dot_nt(grad_v[...], weight_v[q * n : (q + 1) * n, :]).astype(BF)
        back_v[:, q * n : (q + 1) * n] = row[:ROWS]
        for j in range(MAIN // 4):
            at = (q * (MAIN // 4) + j) * EXP
            spare_v[at : at + EXP, :] = row[ROWS:, j * SEG : (j + 1) * SEG]
        outs.append(start(cols(back_v, q * n, n), cols(back_ref, q * n, n), sem_out.at[q]))
        if q == 0:
            for t in range(N_DP):
                piece_v[t, :, :HS] = grad_v[:, t * HS : (t + 1) * HS]
                piece_v[t, :, HS:] = grad_v[:, H + t * HS : H + (t + 1) * HS]
            for d in range(N_DP):
                t = lax.rem(own + d, N_DP)
                outs.append(start(piece_v.at[t], pieces[d], sem_out.at[4 + d]))
    back_v[:, D : D + SEG] = dot(fold_mask(), spare_v[...]).astype(BF)
    high = total.astype(BF)
    low = (total - high.astype(F32)).astype(BF)
    lane = iota((EXP, 128), 1)
    ninth = jnp.where(
        lane == 2,
        high[ROWS:].astype(F32),
        jnp.where(lane == 3, low[ROWS:].astype(F32), 0.0),
    ).astype(BF)
    spread = one((iota((ROWS, EXP), 0) >> 3) == iota((ROWS, EXP), 1)).astype(BF)
    lane_rows = iota((ROWS, 128), 1)
    back_v[:, D + SEG :] = jnp.where(
        lane_rows == 0,
        high[:ROWS].astype(F32),
        jnp.where(lane_rows == 1, low[:ROWS].astype(F32), dot(spread, ninth)),
    ).astype(BF)
    outs.append(start(cols(back_v, D, SEG + 128), cols(back_ref, D, SEG + 128), sem_out.at[8]))
    for copy in outs:
        copy.wait()


def rows_pass(own, recv_dy, down_mat, slope, silu, act, gate_mat, up_mat):
    hbm = pl.BlockSpec(memory_space=pltpu.HBM)
    piece = jax.ShapeDtypeStruct((ALL, 2 * HS), BF)
    return pl.pallas_call(
        rows_kernel,
        in_specs=[pl.BlockSpec(memory_space=pltpu.SMEM)] + [hbm] * 7,
        out_specs=[hbm] * (1 + N_DP),
        out_shape=[jax.ShapeDtypeStruct((ROWS, Y_COLS), BF)] + [piece] * N_DP,
        scratch_shapes=[
            pltpu.VMEM((ALL, D), BF),
            pltpu.VMEM((ROWS, SEG), BF),
            pltpu.VMEM((H, D), BF),
            pltpu.VMEM((ALL, H), F32),
            pltpu.VMEM((ALL, H), F32),
            pltpu.VMEM((ALL, H), F32),
            pltpu.VMEM((D, 2 * H), BF),
            pltpu.VMEM((ALL, 2 * H), BF),
            pltpu.VMEM((N_DP, ALL, 2 * HS), BF),
            pltpu.VMEM((ROWS, Y_COLS), BF),
            pltpu.VMEM((ROWS, SEG), BF),
            pltpu.SemaphoreType.DMA((8,)),
            pltpu.SemaphoreType.DMA((9,)),
        ],
        name="rows_pass",
    )(own, recv_dy, down_mat, slope, silu, act, gate_mat, up_mat)


HALF_H = HS // 2


def down_kernel(
    own_ref, turned_ref, recv_ref, same_ref, next_ref, far_top_ref, far_low_ref, prev_ref,
    rows_v, extra_v, turned_v, out_v, sem_in, sem_out,
):
    ins = [
        start(cols(recv_ref, D, SEG), extra_v, sem_in.at[1]),
        start(cols(recv_ref, 0, D), rows_v.at[pl.ds(0, ROWS)], sem_in.at[0]),
        start(turned_ref, turned_v, sem_in.at[2]),
    ]
    ins[0].wait()
    fill_spare(rows_v, extra_v)
    ins[1].wait()
    ins[2].wait()
    outs = []
    for d in (2, 1, 3, 0):
        at = pl.multiple_of(lax.rem(own_ref[0] + d, N_DP) * HS, HS)
        out_v[d] = dot(turned_v[pl.ds(at, HS), :], rows_v[...]).astype(BF)
        if d == 2:
            top, low = out_v.at[d, pl.ds(0, HALF_H)], out_v.at[d, pl.ds(HALF_H, HALF_H)]
            outs.append(start(top, far_top_ref, sem_out.at[d]))
            outs.append(start(low, far_low_ref, sem_out.at[N_DP]))
        else:
            target = {0: same_ref, 1: next_ref, 3: prev_ref}[d]
            outs.append(start(out_v.at[d], target, sem_out.at[d]))
    for copy in outs:
        copy.wait()


def down_terms(own, turned, recv_dy):
    hbm = pl.BlockSpec(memory_space=pltpu.HBM)
    rows = [HS, HS, HALF_H, HALF_H, HS]
    return pl.pallas_call(
        down_kernel,
        in_specs=[pl.BlockSpec(memory_space=pltpu.SMEM), hbm, hbm],
        out_specs=[hbm] * len(rows),
        out_shape=[jax.ShapeDtypeStruct((n, D), BF) for n in rows],
        scratch_shapes=[
            pltpu.VMEM((ALL, D), BF),
            pltpu.VMEM((ROWS, SEG), BF),
            pltpu.VMEM((H, ALL), BF),
            pltpu.VMEM((N_DP, HS, D), BF),
            pltpu.SemaphoreType.DMA((3,)),
            pltpu.SemaphoreType.DMA((N_DP + 1,)),
        ],
        name="down_terms",
    )(own, turned, recv_dy)


def merge_kernel(next_ref, prev_ref, from_prev_ref, from_next_ref, next_out_ref, prev_out_ref):
    top = next_ref[:HALF_H].astype(F32) + from_prev_ref[...].astype(F32)
    next_out_ref[:HALF_H] = top.astype(BF)
    next_out_ref[HALF_H:] = next_ref[HALF_H:]
    low = prev_ref[HALF_H:].astype(F32) + from_next_ref[...].astype(F32)
    prev_out_ref[:HALF_H] = prev_ref[:HALF_H]
    prev_out_ref[HALF_H:] = low.astype(BF)


def merge(*args):
    shape = jax.ShapeDtypeStruct((HS, D), BF)
    return pl.pallas_call(merge_kernel, out_shape=[shape, shape], name="merge")(*args)


HALF = ROWS // 2
X_PARTS = (1, 2, 2, 2)


def gate_up_kernel(*refs):
    n_x = sum(X_PARTS)
    x_refs, spare_refs, g_refs = refs[:n_x], refs[n_x : 2 * n_x], refs[2 * n_x : 2 * n_x + N_DP]
    gate_ref, up_ref, turned_ref = refs[2 * n_x + N_DP :]
    step = pl.program_id(0)

    @pl.when(step == 0)
    def _():
        for g in range(N_DP):
            turned = g_refs[g][...].astype(F32).T.astype(BF)
            turned_ref[:, g * ROWS : (g + 1) * ROWS] = turned[:, :ROWS]
            turned_ref[:, N_DP * ROWS + g * EXP : N_DP * ROWS + (g + 1) * EXP] = turned[:, ROWS:]

    spares = []
    total = jnp.zeros((2 * HS, SEG), F32)
    at = 0
    for x_ref, spare_ref in zip(x_refs, spare_refs):
        n = x_ref.shape[0]
        pick = one(iota((n // MAIN, n), 1) == iota((n // MAIN, n), 0) * MAIN + step).astype(BF)
        spares.append(dot(pick, spare_ref[...]).astype(BF))
        total = total + dot(turned_ref[:, at : at + n], x_ref[...])
        at += n
    total = total + dot(turned_ref[:, at:], jnp.concatenate(spares, axis=0))
    gate_ref[...] = total[:HS].astype(BF)
    up_ref[...] = total[HS:].astype(BF)


def gate_up_terms(xs, gs):
    mains = [pl.BlockSpec((x.shape[0], SEG), lambda j: (0, j)) for x in xs]
    spares = [pl.BlockSpec((x.shape[0], SEG), lambda j: (0, MAIN)) for x in xs]
    grad = pl.BlockSpec((ALL, 2 * HS), lambda j: (0, 0))
    out = pl.BlockSpec((HS, SEG), lambda j: (0, j))
    shape = jax.ShapeDtypeStruct((HS, D), BF)
    return pl.pallas_call(
        gate_up_kernel,
        grid=(MAIN,),
        in_specs=mains + spares + [grad] * N_DP,
        out_specs=[out, out],
        out_shape=[shape, shape],
        scratch_shapes=[pltpu.VMEM((2 * HS, N_DP * ALL), BF)],
        compiler_params=pltpu.CompilerParams(vmem_limit_bytes=65 * 1024 * 1000),
        name="gate_up_terms",
    )(*xs, *xs, *gs)


def combine_kernel(ids_ref, probs_ref, recv_ref, rows_ref, probs_grad_ref, recv_v, sem):
    tail_in = start(cols(recv_ref, D, SEG + 128), cols(recv_v, D, SEG + 128), sem.at[0])
    main_in = start(cols(recv_ref, 0, D), cols(recv_v, 0, D), sem.at[1])
    ids = jnp.concatenate(
        [ids_ref[...].astype(F32), jnp.zeros((8 - TOP, TOK), F32)], axis=0
    ).T.astype(jnp.int32)
    lane_e = iota((TOK, EXP), 1)
    member = ids[:, 0:1] == lane_e
    for k in range(1, TOP):
        member = member | (ids[:, k : k + 1] == lane_e)
    before = one(iota((TOK, TOK), 1) < iota((TOK, TOK), 0)).astype(BF)
    rank = jnp.where(member, dot(before, one(member).astype(BF)), 200.0)
    slot = iota((TOK, ROWS), 1)
    spread = one(iota((EXP, ROWS), 0) == (iota((EXP, ROWS), 1) >> 3)).astype(BF)
    rank_slots = dot(rank.astype(BF), spread)
    sub = slot & (MAIN - 1)
    main = rank_slots == sub.astype(F32)
    ninth = rank_slots == float(MAIN)
    main_bf = one(main).astype(BF)
    spare = jnp.concatenate([one(ninth & (sub == j)).astype(BF) for j in range(MAIN)], axis=0)
    tail_in.wait()
    extra = dot(spare, recv_v[:, D : D + SEG])
    lanes = one(iota((8, 128), 0) == iota((8, 128), 1)).astype(BF)
    values = dot_nt(lanes, recv_v[:, D + SEG :])
    per_slot = jnp.where(main, values[0:1] + values[1:2], 0.0)
    per_slot = per_slot + jnp.where(ninth & (sub == 0), values[2:3] + values[3:4], 0.0)
    lane_k = iota((TOK, 8), 1)
    found = jnp.zeros((TOK, 8), F32)
    for k in range(TOP):
        hit = ids[:, k : k + 1] == (slot >> 3)
        value = jnp.sum(jnp.where(hit, per_slot, 0.0), axis=1, keepdims=True)
        found = jnp.where(lane_k == k, value, found)
    probs_grad_ref[...] = found.T[:TOP] / probs_ref[...].astype(F32)
    main_in.wait()
    for j in range(MAIN):
        at = slice(j * SEG, (j + 1) * SEG)
        part = dot(main_bf, recv_v[:, at])
        rows_ref[:, at] = (part + extra[j * TOK : (j + 1) * TOK, :]).astype(BF)


def combine(ids, probs, recv):
    vmem = pl.BlockSpec(memory_space=pltpu.VMEM)
    return pl.pallas_call(
        combine_kernel,
        in_specs=[vmem, vmem, pl.BlockSpec(memory_space=pltpu.HBM)],
        out_specs=[vmem, vmem],
        out_shape=[
            jax.ShapeDtypeStruct((TOK, D), BF),
            jax.ShapeDtypeStruct((TOP, TOK), F32),
        ],
        scratch_shapes=[pltpu.VMEM((ROWS, Y_COLS), BF), pltpu.SemaphoreType.DMA((2,))],
        name="combine",
    )(ids, probs, recv)


def exchange(flat):
    out = lax.all_to_all(
        flat.reshape(EXP, MAIN, flat.shape[1]), "expert", split_axis=0, concat_axis=0, tiled=True
    )
    return out.reshape(flat.shape)


def shift(value, by):
    return lax.ppermute(value, "dp", [(i, (i + by) % N_DP) for i in range(N_DP)])


def gather_rows(recv):
    top, low = recv[:HALF], recv[HALF:]
    prev_top = shift(top, 1)
    next_low = shift(low, 3)
    prev_low = shift(low, 1)
    next_top = shift(top, 3)
    far_top = shift(prev_top, 1)
    far_low = shift(next_low, 3)
    return [recv, prev_top, prev_low, far_top, far_low, next_top, next_low]


def per_device(tokens, out_grad, gate_probs, expert_ids, w_gate, w_up, w_down):
    own = lax.axis_index("dp").astype(jnp.int32).reshape(1)
    ids = expert_ids.T
    gate_mat, up_mat, down_mat = w_gate[0], w_up[0], w_down[0]
    recv_x = exchange(pack(pack_x_kernel, ids, tokens))
    probs = gate_probs.T
    recv_dy = exchange(pack(pack_dy_kernel, ids, out_grad, probs))
    xs = gather_rows(recv_x)
    slope, silu, act, turned = forward(recv_x, gate_mat, up_mat)
    back, *pieces = rows_pass(own, recv_dy, down_mat, slope, silu, act, gate_mat, up_mat)
    back_rows = exchange(back)
    gs = [pieces[0]] + [shift(pieces[d], d) for d in range(1, N_DP)]
    terms = down_terms(own, turned, recv_dy)
    own_term, next_term, far_top, far_low, prev_term = terms
    from_prev = shift(far_top, 1)
    from_next = shift(far_low, 3)
    next_term, prev_term = merge(next_term, prev_term, from_prev, from_next)
    downs = [own_term, shift(next_term, 1), shift(prev_term, 3)]
    gate_grad, up_grad = gate_up_terms(xs, gs)
    down_grad = downs[0].astype(F32)
    for term in downs[1:]:
        down_grad = down_grad + term.astype(F32)
    tokens_grad, probs_grad = combine(ids, probs, back_rows)
    return (
        tokens_grad,
        probs_grad.T,
        gate_grad.T[None],
        up_grad.T[None],
        down_grad.astype(BF)[None],
    )


def solution(mesh):
    rows = P(("dp", "expert"), None)
    weights = P("expert", None, None)
    return jax.shard_map(
        per_device,
        mesh=mesh,
        in_specs=(rows, rows, rows, rows, weights, weights, weights),
        out_specs=(rows, rows, P("expert", None, "dp"), P("expert", None, "dp"), P("expert", "dp", None)),
        check_vma=False,
    )
```
